32 devices in a mesh: ax: 8 (over z, y), ty: 2 (over x), tz: 2 (over core).
Axes of the slice: x: 2, y: 2, z: 4, core: 2. Of those that a mesh axis runs over, the one named last changes fastest.
Arguments:
- adjoint: float32 [5, 128, 32, 256], P(None, 'ax', 'ty', 'tz'), may hold values from -6 to 6
- velocity: float32 [3, 128, 32, 256], P(None, 'ax', 'ty', 'tz'), may hold values from -0.5 to 0.5
- sound_speed: float32 [128, 32, 256], P('ax', 'ty', 'tz'), may hold values from 0.6 to 1.2
- sponge: float32 [128, 32, 256], P('ax', 'ty', 'tz'), may hold values from 0.05 to 0.5
- source: float32 [5, 128, 32, 256], P(None, 'ax', 'ty', 'tz'), may hold values from -6 to 6
- mode_basis: float32 [8, 128, 128], P('ax'), may hold values from -0.5 to 0.5
- block_owner: int32 [8, 2, 2, 32, 1], P('ax', 'ty', 'tz'), may hold values from 0 to 7; in each aligned block of 32 rows (0 to 31, 32 to 63, ..., all dimensions but the last counted through in order) at most 8 rows name the same one
Outputs:
- adjoint_out: float32 [5, 128, 32, 256], P(None, 'ax', 'ty', 'tz')
- sensitivity: float32 [8, 5, 128], P('ax', None, ('ty', 'tz'))
The draws below stay inside these ranges and needn't reach their ends.
Inputs may be any that keep to these rules, and one draw needn't show every extreme that they name: `block_owner`: of the 32 face blocks of one brick, at most 8 have the same owner, and in every draw some brick gives exactly 8 to one owner.
All inputs are finite; a program needn't handle non-finite values.
Results may differ from the reference program's by a relative error of at most 0.000092.
Values sent between devices are 32-bit elements; how exact they have to be, the bound alone decides.
No kernel may reach another device: no remote copies, remote signals or barrier semaphores. Data moves between devices by JAX's collectives and lax.ppermute only.
A program may use at most 128 MiB of HBM per device.

```python
import math
import jax
import jax.numpy as jnp
import numpy as np
from jax import lax

CX = 16
CY = 16
CZ = 128
MODES = 128
FACE_PLANES = 2
NX = 128
NY = 32
NZ = 256
CAP = 8
N_AX = 8
N_TY = 2
N_TZ = 2


def level_of(stream_key, dims, cuts, least, top_value):
    gain = 1.0
    for dim, blocks in cuts:
        heights = jax.random.uniform(jax.random.fold_in(jax.random.fold_in(stream_key, 6), dim), (blocks,), jnp.float32, least / len(cuts), top_value / len(cuts))
        gain = gain * jnp.repeat(jnp.exp(heights), dims[dim] // blocks).reshape((-1,) + (1,) * (len(dims) - 1 - dim))
    return gain


def shared_out(stream_key, own, number, rows, amount, top, limit, skew):
    sequence = jax.random.permutation(stream_key, amount)
    crowded, ordinary = portions_of(amount, rows * top, limit, skew, True), portions_of(amount, rows * top, limit, skew, False)
    places = jnp.arange(amount)

    def named(lengths, offset_by):
        used = int((lengths > 0).sum())
        fixed = max(1, used // 4)
        shifted = fixed + (places - fixed + offset_by * (used - fixed)) % max(1, amount - fixed)
        return jnp.zeros((amount,), jnp.int32).at[sequence[jnp.where(places < fixed, places, shifted)]].set(jnp.asarray(lengths, jnp.int32))

    lengths = jnp.where(number % 4 == 0, named(crowded, number // 4), named(ordinary, number - number // 4 - 1))
    mixed = jax.random.permutation(jax.random.fold_in(own, 3), amount)
    donor, receiver = mixed[0:amount // 2 * 2:2], mixed[1:amount // 2 * 2:2]
    slack = jnp.minimum(lengths[donor] - 1, limit - lengths[receiver]) // 2
    slack = jnp.where((donor == sequence[0]) | (receiver == sequence[0]) | (lengths[receiver] == 0), 0, jnp.maximum(slack, 0))
    shifted = jax.random.randint(jax.random.fold_in(own, 4), (amount // 2,), 0, 1 << 20) % (slack + 1)
    lengths = lengths.at[donor].add(-shifted).at[receiver].add(shifted)
    labels = jnp.searchsorted(jnp.cumsum(lengths), jnp.arange(rows * top), side="right").astype(jnp.int32)
    grid = labels.reshape(top, rows).T
    grid = grid[jax.random.permutation(jax.random.fold_in(own, 1), rows)]
    offset_by = jax.random.randint(jax.random.fold_in(own, 2), (rows, 1), 0, top)
    return jnp.take_along_axis(grid, (jnp.arange(top)[None, :] + offset_by) % top, axis=1)


def portions_of(amount, total, most, skew, full):
    portions = [(1 << 20) // math.isqrt(grade ** skew) + 1 for grade in range(1, amount + 1)]
    largest = most if full else min(most, max(-(-total // amount), total * portions[0] // sum(portions)))
    least = 1 if total - largest >= amount - 1 else 0
    given, surplus = [largest] + [least] * (amount - 1), total - largest - least * (amount - 1)
    while surplus > 0:
        candidates = [i for i in range(1, amount) if given[i] < largest] or [i for i in range(1, amount) if given[i] < most]
        mass, budget = sum([portions[i] for i in candidates]), surplus
        for i in candidates:
            addition = min(most - given[i], max(1, budget * portions[i] // mass), surplus)
            given[i] = given[i] + addition
            surplus = surplus - addition
    return np.array(given)


def normal_values(key, shape, width, limit, cuts=(), held_as=jnp.bfloat16):
    drawn = jax.random.normal(key, shape, jnp.float32) * width
    if len(cuts) > 0:
        drawn = level_of(key, shape, cuts, -0.22, 0.18) * drawn
    return jnp.clip(drawn, min=-limit, max=limit).astype(held_as)


def setup_inputs(seed: int = 0) -> dict:
    keys = jax.random.split(jax.random.key(seed), 8)
    adjoint = normal_values(keys[0], (5, NX, NY, NZ), 1.0, 6.0, ((1, 8), (2, 2), (3, 2)), jnp.float32)
    velocity = jnp.clip(jax.random.uniform(keys[1], (3, NX, NY, NZ), jnp.float32, -0.5, 0.5) * level_of(keys[1], (3, NX, NY, NZ), ((1, 8), (2, 2), (3, 2)), -0.4, 0.0), -0.5, 0.5)
    sound_speed = jnp.clip(jnp.exp(math.log(1.2) - 0.6931472 * jax.random.uniform(keys[2], (NX, NY, NZ), jnp.float32) ** level_of(keys[2], (NX, NY, NZ), ((0, 8), (1, 2), (2, 2)), -0.2, 0.2)), 0.6, 1.2)
    sponge = jnp.clip(jnp.exp(math.log(0.5) - 2.3025851 * jax.random.uniform(keys[3], (NX, NY, NZ), jnp.float32) ** level_of(keys[3], (NX, NY, NZ), ((0, 8), (1, 2), (2, 2)), -0.2, 0.2)), 0.05, 0.5)
    source = normal_values(keys[4], (5, NX, NY, NZ), 1.0, 6.0, ((1, 8), (2, 2), (3, 2)), jnp.float32)
    mode_basis = normal_values(keys[5], (N_AX, CZ, MODES), CZ ** -0.5, 0.5, ((0, 8),), jnp.float32)
    block_owner_keys = jax.random.split(jax.random.fold_in(keys[6], 1), N_AX * N_TY * N_TZ * (FACE_PLANES * CY) // (FACE_PLANES * CY))
    block_owner_turns = jax.random.permutation(jax.random.fold_in(keys[6], 3), N_AX * N_TY * N_TZ * (FACE_PLANES * CY) // (FACE_PLANES * CY))
    block_owner = jax.vmap(lambda own, number: shared_out(jax.random.fold_in(keys[6], 2), own, number, FACE_PLANES * CY, N_AX, 1, CAP, 2))(block_owner_keys, block_owner_turns).reshape((N_AX, N_TY, N_TZ, FACE_PLANES * CY, 1))
    return dict(adjoint=adjoint, velocity=velocity, sound_speed=sound_speed, sponge=sponge, source=source, mode_basis=mode_basis, block_owner=block_owner)


time_step = 0.6
weights_fd = (45.0 / 60.0, -9.0 / 60.0, 1.0 / 60.0)

def difference(padded, direction, length):
    summed = None
    for s in range(1, 4):
        forward = lax.slice_in_dim(padded, 3 + s, 3 + s + length, axis=direction)
        backward = lax.slice_in_dim(padded, 3 - s, 3 - s + length, axis=direction)
        contrib = weights_fd[s - 1] * (forward - backward)
        summed = contrib if summed is None else summed + contrib
    return summed

def combine(gradients, velocity, sound_speed, sponge, source, current):
    advect = [velocity[0] * gradients[0][k] + velocity[1] * gradients[1][k] + velocity[2] * gradients[2][k] for k in range(5)]
    pieces = [advect[0]]
    for d in range(3):
        pieces.append(advect[1 + d] + sound_speed * gradients[d][4])
    pieces.append(advect[4] + sound_speed * (gradients[0][1] + gradients[1][2] + gradients[2][3]))
    return jnp.stack(pieces) - sponge * current + source

def rate_of(current, velocity, sound_speed, sponge, source):
    padded = jnp.pad(current, ((0, 0), (3, 3), (3, 3), (3, 3)))
    gradients = []
    for direction in (1, 2, 3):
        trimmed = padded
        for other in (1, 2, 3):
            if other != direction:
                trimmed = lax.slice_in_dim(trimmed, 3, trimmed.shape[other] - 3, axis=other)
        gradients.append(difference(trimmed, direction, current.shape[direction]))
    return combine(gradients, velocity, sound_speed, sponge, source, current)

def reference(adjoint, velocity, sound_speed, sponge, source, mode_basis, block_owner):
    first = rate_of(adjoint, velocity, sound_speed, sponge, source)
    middle = adjoint + time_step * first
    second = rate_of(middle, velocity, sound_speed, sponge, source)
    adjoint_out = adjoint + 0.5 * time_step * (first + second)
    shaped = adjoint_out.reshape(5, N_AX, CX, N_TY, CY, N_TZ, CZ)[:, :, :FACE_PLANES]
    blocks = jnp.transpose(shaped, (1, 3, 5, 2, 4, 0, 6)).reshape(-1, 5, CZ)
    owners = block_owner.reshape(-1)
    onehot = (owners[:, None] == jnp.arange(N_AX, dtype=jnp.int32)[None, :]).astype(jnp.float32)
    gathered = jnp.einsum('bo,bkc->okc', onehot, blocks, precision=lax.Precision.HIGHEST)
    projected = jnp.einsum('okc,ocm->okm', gathered, mode_basis, precision=lax.Precision.HIGHEST)
    sensitivity = projected / math.sqrt(FACE_PLANES * CY * N_TY * N_TZ)
    return (adjoint_out, sensitivity)
```

```python
import functools
import math

import jax
import jax.numpy as jnp
import numpy as np
from jax import lax
from jax.experimental import pallas as pl
from jax.experimental.pallas import tpu as pltpu
from jax.sharding import PartitionSpec as P

FACE_PLANES = 2
TIME_STEP = 0.6
HALO = 3
WEIGHTS = {1: 45.0, 2: -9.0, 3: 1.0}
F32, BF16 = jnp.float32, jnp.bfloat16
VMEM = pl.BlockSpec(memory_space=pltpu.VMEM)
ANY = pl.BlockSpec(memory_space=pl.ANY)


def weight_of(offset):
    size = np.abs(offset)
    table = np.zeros(offset.shape, np.float32)
    for s, w in WEIGHTS.items():
        table = np.where(size == s, np.sign(offset) * w, table)
    return table


def tables(nx, ny, nz):
    y, z, layer, x = np.arange(ny), np.arange(nz), np.arange(HALO), np.eye(nx, dtype=np.float32)
    along_y = np.kron(x, weight_of(y[None, :] - y[:, None]))
    along_z = weight_of(z[:, None] - z[None, :])

    def from_rows(places):
        w = weight_of(places[None, :] - y[:, None])
        m = np.einsum("xp,yl->xylp", x, w)
        return m.reshape(nx * ny, HALO * nx)

    y_halo = np.stack([from_rows(ny + layer), from_rows(layer - HALO), np.zeros((nx * ny, HALO * nx))])
    z_halo = np.stack(
        [weight_of(z[:, None] + nz - z[None, :]), weight_of(z[:, None] - nz - z[None, :]), np.zeros((nz, nz))]
    )
    twice = lambda m, axis: np.concatenate([m, m], axis=axis)
    return [
        jnp.asarray(m, BF16)
        for m in (along_y, twice(along_z, 0), twice(y_halo, 2), twice(z_halo, 1))
    ]


def halves(v):
    high = v.astype(BF16)
    return high, (v - high.astype(F32)).astype(BF16)


def dot(a, b):
    return jnp.dot(a, b, preferred_element_type=F32)


def couple(acc, u, c, d, grad):
    acc = [acc[k] + u * grad[k] for k in range(5)]
    acc[1 + d] = acc[1 + d] + c * grad[4]
    acc[4] = acc[4] + c * grad[1 + d]
    return acc


def pack(v_ref, xlo_ref, xhi_ref, y_refs, position, count):
    nx, ny = v_ref.shape[1:3]
    xlo_ref[...] = v_ref[:, :HALO]
    xhi_ref[...] = v_ref[:, nx - HALO :]

    def rows(ref, start):
        for k in range(5):
            for l in range(HALO):
                ref[k, l] = v_ref[k, :, start + l, :]

    if count == 2:

        @pl.when(position == 0)
        def _():
            rows(y_refs[0], ny - HALO)

        @pl.when(position != 0)
        def _():
            rows(y_refs[0], 0)
    else:
        rows(y_refs[0], 0)
        rows(y_refs[1], ny - HALO)


def pack_kernel(count, v_ref, xlo_ref, xhi_ref, *y_refs):
    pack(v_ref, xlo_ref, xhi_ref, y_refs, lax.axis_index("ty"), count)


def local_kernel(scale, second, *refs):
    if second:
        _, adj_ref, v_ref, vel_ref, c_ref, sponge_ref, source_ref, ay_ref, bz_ref, out_ref, dy, dz = refs
    else:
        _, v_ref, vel_ref, c_ref, sponge_ref, source_ref, ay_ref, bz_ref, out_ref, dy, dz = refs
        adj_ref = None
    nx, ny, nz = v_ref.shape[1:]
    for k in range(5):
        high, low = halves(v_ref[k].reshape(nx * ny, nz))
        dz[k] = dot(jnp.concatenate([high, low], axis=1), bz_ref[...]).reshape(nx, ny, nz)
        dy[k] = (dot(ay_ref[...], high) + dot(ay_ref[...], low)).reshape(nx, ny, nz)
    part = scale / 60.0
    for x in range(nx):
        c = c_ref[x] * part
        u = [vel_ref[d, x] * part for d in range(3)]
        damp = sponge_ref[x] * scale
        acc, gx, gy, gz = [], [], [], []
        for k in range(5):
            cur = v_ref[k, x]
            base = cur if adj_ref is None else 0.5 * (adj_ref[k, x] + cur)
            acc.append(base + (scale * source_ref[k, x] - damp * cur))
            total = None
            for s, w in WEIGHTS.items():
                diff = None
                if x + s < nx and x - s >= 0:
                    diff = v_ref[k, x + s] - v_ref[k, x - s]
                elif x + s < nx:
                    diff = v_ref[k, x + s]
                elif x - s >= 0:
                    diff = -v_ref[k, x - s]
                if diff is not None:
                    diff = diff if w == 1.0 else w * diff
                    total = diff if total is None else total + diff
            gx.append(total)
            gy.append(dy[k, x])
            gz.append(dz[k, x])
        for d, g in enumerate((gx, gy, gz)):
            acc = couple(acc, u[d], c, d, g)
        for k in range(5):
            out_ref[k, x] = acc[k]


def edge_flags():
    at, count = lax.axis_index("ax"), lax.axis_size("ax")
    return (at > 0).astype(F32), (at < count - 1).astype(F32)


def side_of(axis):
    at, count = lax.axis_index(axis), lax.axis_size(axis)
    if count == 2:
        return [at]
    return [jnp.where(at > 0, 1, 2), jnp.where(at < count - 1, 0, 2)]


def add_halos(scale, part_ref, vel_ref, c_ref, from_lo, from_hi, y_blocks, z_blocks, py_ref, wz_ref, dy, dz, out_ref):
    nx, ny, nz = part_ref.shape[1:]
    y_sides, z_sides = side_of("ty"), side_of("tz")
    has_lo, has_hi = edge_flags()
    for k in range(5):
        total = None
        for ref, side in zip(y_blocks, y_sides):
            high, low = halves(ref[k].reshape(HALO * nx, nz))
            term = dot(py_ref[side], jnp.concatenate([high, low], axis=0))
            total = term if total is None else total + term
        dy[k] = total.reshape(nx, ny, nz)
        total = None
        for ref, side in zip(z_blocks, z_sides):
            high, low = halves(ref[k].reshape(nx * ny, nz))
            term = dot(jnp.concatenate([high, low], axis=1), wz_ref[side])
            total = term if total is None else total + term
        dz[k] = total.reshape(nx, ny, nz)
    part = scale / 60.0
    for x in range(nx):
        c = c_ref[x] * part
        acc = [part_ref[k, x] for k in range(5)]
        for ref, has, places in ((from_lo, has_lo, range(-HALO, 0)), (from_hi, has_hi, range(nx, nx + HALO))):
            near = [(l, p - x) for l, p in enumerate(places) if abs(p - x) <= HALO]
            if near:
                grad = []
                for k in range(5):
                    total = None
                    for l, off in near:
                        w = WEIGHTS[abs(off)] * (1.0 if off > 0 else -1.0)
                        term = ref[k, l] * w
                        total = term if total is None else total + term
                    grad.append(total)
                keep = part * has
                acc = couple(acc, vel_ref[0, x] * keep, c_ref[x] * keep, 0, grad)
        acc = couple(acc, vel_ref[1, x] * part, c, 1, [dy[k, x] for k in range(5)])
        acc = couple(acc, vel_ref[2, x] * part, c, 2, [dz[k, x] for k in range(5)])
        for k in range(5):
            out_ref[k, x] = acc[k]


def halo_kernel(scale, ny_blocks, nz_blocks, last, *refs):
    refs = list(refs)
    part_ref, vel_ref, c_ref, from_lo, from_hi = refs[:5]
    y_blocks, refs = refs[5 : 5 + ny_blocks], refs[5 + ny_blocks :]
    z_blocks, refs = refs[:nz_blocks], refs[nz_blocks:]
    if last:
        py_ref, wz_ref, owner_ref, out_ref, sums_ref, dy, dz = refs
    else:
        py_ref, wz_ref, out_ref, xlo_ref, xhi_ref = refs[:5]
        y_refs, (dy, dz) = refs[5:-2], refs[-2:]
    add_halos(scale, part_ref, vel_ref, c_ref, from_lo, from_hi, y_blocks, z_blocks, py_ref, wz_ref, dy, dz, out_ref)
    if not last:
        pack(out_ref, xlo_ref, xhi_ref, y_refs, lax.axis_index("ty"), lax.axis_size("ty"))
        return
    ny, nz = out_ref.shape[2:]
    devices = sums_ref.shape[0]
    each = devices // lax.axis_size("ax")
    blocks = FACE_PLANES * ny
    place = lax.broadcasted_iota(jnp.int32, (blocks, devices), 1) // each
    choose = (owner_ref[...] == place).astype(F32)
    sums_ref[...] = jnp.zeros(sums_ref.shape, F32)
    for k in range(5):
        rows = out_ref[k, :FACE_PLANES].reshape(blocks, nz)
        sums_ref[:, k, :] = lax.dot_general(
            choose, rows, (((0,), (0,)), ((), ())), precision=lax.Precision.HIGHEST, preferred_element_type=F32
        )


def modes_kernel(scale, sums_ref, basis_ref, out_ref):
    share = out_ref.shape[2]
    total = sums_ref[0]
    for i in range(1, sums_ref.shape[0]):
        total = total + sums_ref[i]
    modes = lax.dot_general(
        total, basis_ref[0], (((1,), (0,)), ((), ())), precision=lax.Precision.HIGHEST, preferred_element_type=F32
    )
    mine = lax.axis_index("ty") * lax.axis_size("tz") + lax.axis_index("tz")
    width = modes.shape[1]
    modes = pltpu.roll(modes * scale, lax.rem(width - mine * share, width), 1)
    out_ref[0] = modes[:5, :share]


def ring(v, axis, step):
    count = lax.axis_size(axis)
    return lax.ppermute(v, axis, [(i, (i + step) % count) for i in range(count)])


def exchange(v, xlo, xhi, ys):
    below, above = ring(xhi, "ax", 1), ring(xlo, "ax", -1)
    if lax.axis_size("ty") == 2:
        y_blocks = [ring(ys[0], "ty", 1)]
    else:
        y_blocks = [ring(ys[1], "ty", 1), ring(ys[0], "ty", -1)]
    if lax.axis_size("tz") == 2:
        z_blocks = [ring(v, "tz", 1)]
    else:
        z_blocks = [ring(v, "tz", 1), ring(v, "tz", -1)]
    return below, above, y_blocks, z_blocks


def call(kernel, args, outs, scratch=(), specs=None, flops=0):
    moved = sum(4 * math.prod(a.shape) for a in (*args, *outs))
    return pl.pallas_call(
        kernel,
        out_shape=list(outs),
        in_specs=specs or [VMEM] * len(args),
        out_specs=[VMEM] * len(outs),
        scratch_shapes=list(scratch),
        cost_estimate=pl.CostEstimate(flops=flops, bytes_accessed=moved, transcendentals=0),
        compiler_params=pltpu.CompilerParams(vmem_limit_bytes=48 << 20),
    )(*args)


def on_device(adjoint, velocity, sound_speed, sponge, source, mode_basis, block_owner):
    nx, ny, nz = adjoint.shape[1:]
    n_ax, n_ty, n_tz = (lax.axis_size(a) for a in ("ax", "ty", "tz"))
    ay, bz, py, wz = tables(nx, ny, nz)
    shape = lambda *s: jax.ShapeDtypeStruct(s, F32)
    brick = shape(5, nx, ny, nz)
    side_x, side_y = shape(5, HALO, ny, nz), shape(5, HALO, nx, nz)
    sides = [side_x, side_x] + [side_y] * (1 if n_ty == 2 else 2)
    grads = [pltpu.VMEM((5, nx, ny, nz), F32)] * 2
    work = 5 * nx * ny * nz * 800

    xlo, xhi, *ys = call(functools.partial(pack_kernel, n_ty), [adjoint], sides)
    below, above, y_blocks, z_blocks = exchange(adjoint, xlo, xhi, ys)
    rest = [velocity, sound_speed, sponge, source, ay, bz]
    args = [xlo, adjoint, *rest]
    (part,) = call(
        functools.partial(local_kernel, TIME_STEP, False), args, [brick], grads, [ANY] + [VMEM] * (len(args) - 1), work
    )
    args = [part, velocity, sound_speed, below, above, *y_blocks, *z_blocks, py, wz]
    mid, xlo, xhi, *ys = call(
        functools.partial(halo_kernel, TIME_STEP, len(y_blocks), len(z_blocks), False),
        args,
        [brick, *sides],
        grads,
        flops=work // 2,
    )
    below, above, y_blocks, z_blocks = exchange(mid, xlo, xhi, ys)
    args = [xlo, adjoint, mid, *rest]
    (part,) = call(
        functools.partial(local_kernel, 0.5 * TIME_STEP, True), args, [brick], grads, [ANY] + [VMEM] * (len(args) - 1), work
    )
    devices = n_ax * n_ty * n_tz
    owners = block_owner.reshape(FACE_PLANES * ny, 1)
    args = [part, velocity, sound_speed, below, above, *y_blocks, *z_blocks, py, wz, owners]
    adjoint_out, sums = call(
        functools.partial(halo_kernel, 0.5 * TIME_STEP, len(y_blocks), len(z_blocks), True),
        args,
        [brick, shape(devices, 8, nz)],
        grads,
        flops=work // 2,
    )
    sums = lax.all_to_all(sums, ("ax", "ty", "tz"), split_axis=0, concat_axis=0, tiled=True)
    share = mode_basis.shape[2] // (n_ty * n_tz)
    scale = 1.0 / math.sqrt(FACE_PLANES * ny * n_ty * n_tz)
    (sensitivity,) = call(functools.partial(modes_kernel, scale), [sums, mode_basis], [shape(1, 5, share)])
    return (adjoint_out, sensitivity)


def solution(mesh):
    return jax.shard_map(
        on_device,
        mesh=mesh,
        in_specs=(
            P(None, "ax", "ty", "tz"),
            P(None, "ax", "ty", "tz"),
            P("ax", "ty", "tz"),
            P("ax", "ty", "tz"),
            P(None, "ax", "ty", "tz"),
            P("ax", None, None),
            P("ax", "ty", "tz", None, None),
        ),
        out_specs=(P(None, "ax", "ty", "tz"), P("ax", None, ("ty", "tz"))),
        check_vma=False,
    )
```

```python
import functools
import math

import jax
import jax.numpy as jnp
import numpy as np
from jax import lax
from jax.experimental import pallas as pl
from jax.experimental.pallas import tpu as pltpu
from jax.sharding import PartitionSpec as P

FACE_PLANES = 2
TIME_STEP = 0.6
HALO = 3
WEIGHTS = {1: 45.0, 2: -9.0, 3: 1.0}
F32, BF16 = jnp.float32, jnp.bfloat16
VMEM = pl.BlockSpec(memory_space=pltpu.VMEM)
ANY = pl.BlockSpec(memory_space=pl.ANY)
HBM = pl.BlockSpec(memory_space=pltpu.HBM)
ABOVE, BELOW, NONE = 0, 1, 2


def weight_of(offset):
    size = np.abs(offset)
    table = np.zeros(offset.shape, np.float32)
    for s, w in WEIGHTS.items():
        table = np.where(size == s, np.sign(offset) * w, table)
    return table


def tables(nx, ny, nz):
    y, z, layer, x = np.arange(ny), np.arange(nz), np.arange(HALO), np.eye(nx, dtype=np.float32)
    face = np.eye(FACE_PLANES, dtype=np.float32)
    band = weight_of(y[None, :] - y[:, None])
    along_z = weight_of(z[:, None] - z[None, :])

    def from_rows(places):
        w = weight_of(places[None, :] - y[:, None])
        return np.einsum("xp,yl->xylp", x, w).reshape(nx * ny, HALO * nx)

    y_halo = np.stack([from_rows(ny + layer), from_rows(layer - HALO), np.zeros((nx * ny, HALO * nx))])
    y_face = np.stack(
        [np.kron(face, weight_of(y[None, :] + o - y[:, None])) for o in (ny, -ny)]
        + [np.zeros((FACE_PLANES * ny, FACE_PLANES * ny))]
    )
    z_halo = np.stack([weight_of(z[:, None] + o - z[None, :]) for o in (nz, -nz)] + [np.zeros((nz, nz))])
    twice = lambda m, axis: np.concatenate([m, m], axis=axis)
    return dict(
        ay=jnp.asarray(np.kron(x, band), BF16),
        bz=jnp.asarray(twice(along_z, 0), BF16),
        py=jnp.asarray(twice(y_halo, 2), BF16),
        wz=jnp.asarray(twice(z_halo, 1), BF16),
        fy=jnp.asarray(np.concatenate([twice(np.kron(face, band), 1)[None], twice(y_face, 2)]), BF16),
    )


def halves(v):
    high = v.astype(BF16)
    return high, (v - high.astype(F32)).astype(BF16)


def stacked(v, axis):
    return jnp.concatenate(halves(v), axis=axis)


def dot(a, b):
    return jnp.dot(a, b, preferred_element_type=F32)


def couple(acc, u, c, d, grad):
    acc = [u * grad[k] if acc is None else acc[k] + u * grad[k] for k in range(5)]
    acc[1 + d] = acc[1 + d] + c * grad[4]
    acc[4] = acc[4] + c * grad[1 + d]
    return acc


def pairs_of(count):
    return count % 2 == 0


def x_sides():
    at, count = lax.axis_index("ax"), lax.axis_size("ax")
    has_lo, has_hi = at > 0, at < count - 1
    if not pairs_of(count):
        return [(False, has_lo), (True, has_hi)]
    even = lax.rem(at, 2) == 0
    return [(even, jnp.where(even, has_hi, has_lo)), (jnp.logical_not(even), jnp.where(even, has_lo, has_hi))]


def sides_of(axis):
    at, count = lax.axis_index(axis), lax.axis_size(axis)
    if count == 2:
        return [at]
    return [jnp.where(at > 0, BELOW, NONE), jnp.where(at < count - 1, ABOVE, NONE)]


def turned(side):
    if isinstance(side, int):
        return (BELOW, ABOVE, NONE)[side]
    return jnp.where(side == NONE, NONE, 1 - side)


def start_of(from_above_next, size):
    if isinstance(from_above_next, bool):
        return size - HALO if from_above_next else 0
    return jnp.where(from_above_next, size - HALO, 0)


def pack_first(adj, vel, c, owner_ref, *refs):
    n_y = len(sides_of("ty"))
    x_msgs, y_msgs, (aux, token, rows, sems) = refs[:2], refs[2 : 2 + n_y], refs[2 + n_y :]
    token[...] = jnp.zeros(token.shape, F32)
    nx, ny, nz = adj.shape[1:]
    half = rows.shape[3]
    at = lax.axis_index("ty")
    copies = []

    def copy(src, dst):
        copies.append(pltpu.make_async_copy(src, dst, sems.at[len(copies)]))
        copies[-1].start()

    if n_y == 1:
        tops = [at == 0]
    else:
        tops = [True, False]
    for i, top in enumerate(tops):
        first = (ny - half if top else 0) if isinstance(top, bool) else pl.multiple_of(jnp.where(top, ny - half, 0), 8)
        copy(adj.at[:, :, pl.ds(first, half), :], rows.at[i])
    for ref, (above, _) in zip(x_msgs, x_sides()):
        up = above if pairs_of(lax.axis_size("ax")) else not above
        copy(adj.at[:, pl.ds(start_of(up, nx), HALO)], ref.at[:5])
    for d, msgs in enumerate((x_msgs, y_msgs, (aux,))):
        for ref in msgs:
            n = ref.shape[0]
            copy(vel.at[d, :FACE_PLANES], ref.at[n - 2, :2])
            copy(c.at[0], ref.at[n - 2, 2])
            copy(c.at[1], ref.at[n - 1, 0])
    blocks = owner_ref.shape[1]
    eye = lax.broadcasted_iota(jnp.int32, (blocks, blocks), 0) == lax.broadcasted_iota(jnp.int32, (blocks, blocks), 1)
    column = jnp.sum(jnp.where(eye, owner_ref[...].astype(F32), 0.0), axis=1, keepdims=True)
    owners = jnp.broadcast_to(column, (blocks, nz)).reshape(FACE_PLANES, ny, nz)
    for ref in (*x_msgs, *y_msgs, aux):
        ref[ref.shape[0] - 1, 1:] = owners
    for one in copies:
        one.wait()
    for i, (ref, top) in enumerate(zip(y_msgs, tops)):

        def put(r, ref=ref, i=i):
            for k in range(5):
                for l in range(HALO):
                    ref[k, l] = rows[i, k, :, r + l, :]

        if isinstance(top, bool):
            put(half - HALO if top else 0)
        else:
            pl.when(top)(functools.partial(put, half - HALO))
            pl.when(jnp.logical_not(top))(functools.partial(put, 0))


def pack_second(v_ref, x_msgs, y_msgs):
    nx, ny = v_ref.shape[1:3]
    for ref, (above, _) in zip(x_msgs, x_sides()):
        up = above if pairs_of(lax.axis_size("ax")) else not above
        ref[...] = v_ref[:, pl.ds(start_of(up, nx), HALO)]

    def put(ref, start):
        for k in range(5):
            for l in range(HALO):
                ref[k, l] = v_ref[k, :, start + l, :]

    if len(y_msgs) == 1:
        at = lax.axis_index("ty")
        pl.when(at == 0)(functools.partial(put, y_msgs[0], ny - HALO))
        pl.when(at != 0)(functools.partial(put, y_msgs[0], 0))
    else:
        put(y_msgs[0], ny - HALO)
        put(y_msgs[1], 0)


def x_difference(v_ref, k, x):
    nx, total = v_ref.shape[1], None
    for s, w in WEIGHTS.items():
        diff = None
        if x + s < nx:
            diff = v_ref[k, x + s]
        if x - s >= 0:
            diff = -v_ref[k, x - s] if diff is None else diff - v_ref[k, x - s]
        if diff is not None:
            diff = diff if w == 1.0 else w * diff
            total = diff if total is None else total + diff
    return total


def own_rate(scale, x, v_ref, adj_ref, vel_ref, c_ref, sponge_ref, source_ref, gy, gz):
    part = scale / 60.0
    c, damp = c_ref[x] * part, sponge_ref[x] * scale
    acc = []
    for k in range(5):
        cur = v_ref[k, x]
        base = cur if adj_ref is None else 0.5 * (adj_ref[k, x] + cur)
        acc.append(base + (scale * source_ref[k, x] - damp * cur))
    gx = [x_difference(v_ref, k, x) for k in range(5)]
    for d, g in enumerate((gx, gy, gz)):
        acc = couple(acc, vel_ref[d, x] * part, c, d, g)
    return acc


def own_differences(v_ref, ay_ref, bz_ref, k):
    nx, ny, nz = v_ref.shape[1:]
    high, low = halves(v_ref[k].reshape(nx * ny, nz))
    along_z = dot(jnp.concatenate([high, low], axis=1), bz_ref[...])
    return dot(ay_ref[...], high) + dot(ay_ref[...], low), along_z


def halo_differences(k, shape, y_blocks, z_blocks, py_ref, wz_ref, along_y=None, along_z=None):
    nx, ny, nz = shape
    for ref, side in zip(y_blocks, sides_of("ty")):
        term = dot(py_ref[side], stacked(ref[k].reshape(HALO * nx, nz), 0))
        along_y = term if along_y is None else along_y + term
    for ref, side in zip(z_blocks, sides_of("tz")):
        term = dot(stacked(ref[k].reshape(nx * ny, nz), 1), wz_ref[side])
        along_z = term if along_z is None else along_z + term
    return along_y, along_z


def add_x_blocks(scale, out_ref, vel_ref, c_ref, x_blocks):
    nx = out_ref.shape[1]
    for ref, (above, present) in zip(x_blocks, x_sides()):
        keep = jnp.where(present, jnp.where(above, scale / 60.0, -scale / 60.0), 0.0)
        for e in range(HALO):
            x = jnp.where(above, nx - 1 - e, e)
            grad = []
            for k in range(5):
                total = None
                for m in range(HALO - e):
                    w = WEIGHTS[m + 1 + e]
                    term = ref[k, jnp.where(above, m, HALO - 1 - m)]
                    term = term if w == 1.0 else w * term
                    total = term if total is None else total + term
                grad.append(total)
            acc = couple([out_ref[k, x] for k in range(5)], vel_ref[0, x] * keep, c_ref[x] * keep, 0, grad)
            for k in range(5):
                out_ref[k, x] = acc[k]


def local_kernel(scale, v_ref, vel_ref, c_ref, sponge_ref, source_ref, ay_ref, bz_ref, _, out_ref, dy, dz):
    nx, ny, nz = v_ref.shape[1:]
    for k in range(5):
        along_y, along_z = own_differences(v_ref, ay_ref, bz_ref, k)
        dy[k], dz[k] = along_y.reshape(nx, ny, nz), along_z.reshape(nx, ny, nz)
    for x in range(nx):
        gy, gz = [dy[k, x] for k in range(5)], [dz[k, x] for k in range(5)]
        acc = own_rate(scale, x, v_ref, None, vel_ref, c_ref, sponge_ref, source_ref, gy, gz)
        for k in range(5):
            out_ref[k, x] = acc[k]


def face_sums(scale, mid, adj, vel, c, sponge, source, x_blocks, y_blocks, auxes, owner_ref, bz, wz, fy, sums_ref):
    nx, ny, nz = mid.shape[1:]
    rows = FACE_PLANES * ny
    part = scale / 60.0
    flat = lambda v: v.reshape(rows, nz)
    tall, wide = [], []
    for k in range(5):
        high, low = halves(flat(mid[k, :FACE_PLANES]))
        tall.append(jnp.concatenate([high, low], axis=0))
        wide.append(jnp.concatenate([high, low], axis=1))
    groups, owners = [], []
    gy = [dot(fy[0], tall[k]).reshape(FACE_PLANES, ny, nz) for k in range(5)]
    gz = [dot(wide[k], bz[...]).reshape(FACE_PLANES, ny, nz) for k in range(5)]
    planes = [
        own_rate(scale, p, mid, adj, vel, c, sponge, source, [g[p] for g in gy], [g[p] for g in gz])
        for p in range(FACE_PLANES)
    ]
    groups.append([jnp.concatenate([planes[p][k] for p in range(FACE_PLANES)], axis=0) for k in range(5)])
    owners.append(owner_ref[...].astype(F32))

    def neighbour(ref, d, keep, grad):
        n = ref.shape[0]
        u = flat(ref[n - 2, :2])
        speed = jnp.concatenate([ref[n - 2, 2], ref[n - 1, 0]], axis=0)
        groups.append(couple(None, u * keep, speed * keep, d, grad))
        owners.append(flat(ref[n - 1, 1:])[:, :1])

    grad = []
    for k in range(5):
        at_plane = []
        for p in range(FACE_PLANES):
            total = None
            for l in range(p, HALO):
                w = WEIGHTS[HALO + p - l]
                term = mid[k, nx - HALO + l]
                term = term if w == 1.0 else w * term
                total = term if total is None else total + term
            at_plane.append(total)
        grad.append(jnp.concatenate(at_plane, axis=0))
    for ref, (above, present) in zip(x_blocks, x_sides()):
        keep = jnp.where(jnp.logical_and(above, present), -part, 0.0)
        neighbour(ref, 0, keep, grad)
    for ref, side in zip(y_blocks, sides_of("ty")):
        neighbour(ref, 1, part, [dot(fy[1 + turned(side)], tall[k]) for k in range(5)])
    for ref, side in zip(auxes, sides_of("tz")):
        neighbour(ref, 2, part, [dot(wide[k], wz[turned(side)]) for k in range(5)])

    devices = sums_ref.shape[0]
    each = devices // lax.axis_size("ax")
    blocks = owner_ref.shape[1]
    eye = lax.broadcasted_iota(jnp.int32, (blocks, blocks), 0) == lax.broadcasted_iota(jnp.int32, (blocks, blocks), 1)
    owners[0] = jnp.sum(jnp.where(eye, owners[0], 0.0), axis=1, keepdims=True)
    total = rows * len(groups)
    place = (lax.broadcasted_iota(jnp.int32, (total, devices), 1) // each).astype(F32)
    choose = (jnp.concatenate(owners, axis=0) == place).astype(F32).astype(BF16)
    choose = jnp.concatenate([choose, choose], axis=0)
    sums_ref[:, 5:, :] = jnp.zeros((devices, sums_ref.shape[1] - 5, nz), F32)
    for k in range(5):
        values = stacked(jnp.concatenate([g[k] for g in groups], axis=0), 0)
        sums_ref[:, k, :] = lax.dot_general(choose, values, (((0,), (0,)), ((), ())), preferred_element_type=F32)


def mid_kernel(*refs):
    refs = list(refs)
    n_y, n_z = len(sides_of("ty")), len(sides_of("tz"))
    part_ref, adj, vel, c, sponge, source, owner_ref, bz, py, wz, fy = refs[:11]
    x_blocks, refs = refs[11:13], refs[13:]
    y_blocks, z_blocks, auxes, refs = refs[:n_y], refs[n_y : n_y + n_z], refs[n_y + n_z : n_y + 2 * n_z], refs[n_y + 2 * n_z :]
    out_ref, sums_ref, x_msgs, y_msgs, dy, dz = refs[0], refs[1], refs[2:4], refs[4 : 4 + n_y], refs[-2], refs[-1]
    shape = nx, ny, nz = out_ref.shape[1:]
    for k in range(5):
        along_y, along_z = halo_differences(k, shape, y_blocks, z_blocks, py, wz)
        dy[k], dz[k] = along_y.reshape(shape), along_z.reshape(shape)
    part = TIME_STEP / 60.0
    for x in range(nx):
        acc, speed = [part_ref[k, x] for k in range(5)], c[x] * part
        acc = couple(acc, vel[1, x] * part, speed, 1, [dy[k, x] for k in range(5)])
        acc = couple(acc, vel[2, x] * part, speed, 2, [dz[k, x] for k in range(5)])
        for k in range(5):
            out_ref[k, x] = acc[k]
    add_x_blocks(TIME_STEP, out_ref, vel, c, x_blocks)
    pack_second(out_ref, x_msgs, y_msgs)
    face_sums(
        0.5 * TIME_STEP, out_ref, adj, vel, c, sponge, source, x_blocks, y_blocks, auxes, owner_ref, bz, wz, fy, sums_ref
    )


def final_kernel(*refs):
    refs = list(refs)
    n_y, n_z = len(sides_of("ty")), len(sides_of("tz"))
    adj, mid, vel, c, sponge, source, ay, bz, py, wz, _ = refs[:11]
    x_blocks, refs = refs[11:13], refs[13:]
    y_blocks, z_blocks, (out_ref, dy, dz) = refs[:n_y], refs[n_y : n_y + n_z], refs[n_y + n_z :]
    shape = nx, ny, nz = out_ref.shape[1:]
    for k in range(5):
        own = own_differences(mid, ay, bz, k)
        along_y, along_z = halo_differences(k, shape, y_blocks, z_blocks, py, wz, *own)
        dy[k], dz[k] = along_y.reshape(shape), along_z.reshape(shape)
    scale = 0.5 * TIME_STEP
    for x in range(nx):
        gy, gz = [dy[k, x] for k in range(5)], [dz[k, x] for k in range(5)]
        acc = own_rate(scale, x, mid, adj, vel, c, sponge, source, gy, gz)
        for k in range(5):
            out_ref[k, x] = acc[k]
    add_x_blocks(scale, out_ref, vel, c, x_blocks)


def modes_kernel(scale, sums_ref, basis_ref, out_ref):
    share = out_ref.shape[2]
    total = sums_ref[0]
    for i in range(1, sums_ref.shape[0]):
        total = total + sums_ref[i]
    modes = lax.dot_general(
        total, basis_ref[0], (((1,), (0,)), ((), ())), precision=lax.Precision.HIGHEST, preferred_element_type=F32
    )
    mine = lax.axis_index("ty") * lax.axis_size("tz") + lax.axis_index("tz")
    width = modes.shape[1]
    modes = pltpu.roll(modes * scale, lax.rem(width - mine * share, width), 1)
    for k in range(5):
        out_ref[k] = modes[k : k + 1, :share]


def swap_x(first, second):
    count, cores = lax.axis_size("ax"), lax.axis_size("tz")
    if not pairs_of(count):
        return [ring(first, "ax", 1), ring(second, "ax", -1)]
    near = lax.ppermute(first, "ax", [(i, i ^ 1) for i in range(count)])
    pairs = []
    for i in range(count):
        for u in range(cores):
            if i in (0, count - 1):
                pairs.append((i * cores + u, i * cores + (u + 1) % cores))
            else:
                j = i - 1 if i % 2 == 0 else i + 1
                pairs.append((i * cores + u, j * cores + u))
    return [near, lax.ppermute(second, ("ax", "tz"), pairs)]


def ring(v, axis, step):
    count = lax.axis_size(axis)
    return lax.ppermute(v, axis, [(i, (i + step) % count) for i in range(count)])


def from_sides(axis, to_above, to_below):
    if lax.axis_size(axis) == 2:
        return [ring(to_above, axis, 1)]
    return [ring(to_above, axis, 1), ring(to_below, axis, -1)]


def call(kernel, args, outs, scratch=(), away={}, flops=0, grant=12):
    moved = sum(4 * math.prod(a.shape) for a in (*args, *outs))
    return pl.pallas_call(
        kernel,
        out_shape=list(outs),
        in_specs=[away.get(i, VMEM) for i in range(len(args))],
        out_specs=[VMEM] * len(outs),
        scratch_shapes=list(scratch),
        cost_estimate=pl.CostEstimate(flops=flops, bytes_accessed=moved, transcendentals=0),
        compiler_params=pltpu.CompilerParams(vmem_limit_bytes=grant << 20),
    )(*args)


def on_device(adjoint, velocity, sound_speed, sponge, source, mode_basis, block_owner):
    nx, ny, nz = adjoint.shape[1:]
    n_ax, n_ty, n_tz = (lax.axis_size(a) for a in ("ax", "ty", "tz"))
    n_y = 1 if n_ty == 2 else 2
    t = tables(nx, ny, nz)
    shape = lambda *s: jax.ShapeDtypeStruct(s, F32)
    brick = shape(5, nx, ny, nz)
    grads = [pltpu.VMEM((5, nx, ny, nz), F32)] * 2
    work = 5 * nx * ny * nz * 800
    owners = block_owner.reshape(1, FACE_PLANES * ny)
    devices = n_ax * n_ty * n_tz

    *msgs, aux, token = call(
        pack_first,
        [adjoint, velocity, sound_speed, owners],
        [shape(7, HALO, ny, nz)] * 2 + [shape(7, HALO, nx, nz)] * n_y + [shape(2, HALO, ny, nz), shape(8, nz)],
        [pltpu.VMEM((n_y, 5, nx, 8, nz), F32), pltpu.SemaphoreType.DMA((32,))],
        away={0: HBM, 1: HBM, 2: HBM},
        grant=62,
    )
    z_blocks = from_sides("tz", adjoint, adjoint)
    auxes = from_sides("tz", aux, aux)
    y_blocks = from_sides("ty", msgs[2], msgs[-1])
    x_blocks = swap_x(msgs[0], msgs[1])
    fields = [velocity, sound_speed, sponge, source]
    (part,) = call(
        functools.partial(local_kernel, TIME_STEP),
        [adjoint, *fields, t["ay"], t["bz"], token],
        [brick],
        grads,
        away={7: ANY},
        flops=work,
    )
    mid, sums, *msgs = call(
        mid_kernel,
        [part, adjoint, *fields, owners, t["bz"], t["py"], t["wz"], t["fy"], *x_blocks, *y_blocks, *z_blocks, *auxes],
        [brick, shape(devices, 8, nz)] + [shape(5, HALO, ny, nz)] * 2 + [shape(5, HALO, nx, nz)] * n_y,
        grads,
        flops=work // 2,
        grant=8,
    )
    z_blocks = from_sides("tz", mid, mid)
    y_blocks = from_sides("ty", msgs[2], msgs[-1])
    x_blocks = swap_x(msgs[0], msgs[1])
    sums = lax.all_to_all(sums, ("ax", "ty", "tz"), split_axis=0, concat_axis=0, tiled=True)
    share = mode_basis.shape[2] // (n_ty * n_tz)
    scale = 1.0 / math.sqrt(FACE_PLANES * ny * n_ty * n_tz)
    (modes,) = call(functools.partial(modes_kernel, scale), [sums, mode_basis], [shape(5, 1, share)], grant=2)
    (adjoint_out,) = call(
        final_kernel,
        [adjoint, mid, *fields, t["ay"], t["bz"], t["py"], t["wz"], sums, *x_blocks, *y_blocks, *z_blocks],
        [brick],
        grads,
        away={10: ANY},
        flops=work,
        grant=6,
    )
    return (adjoint_out, jnp.transpose(modes, (1, 0, 2)))


def solution(mesh):
    return jax.shard_map(
        on_device,
        mesh=mesh,
        in_specs=(
            P(None, "ax", "ty", "tz"),
            P(None, "ax", "ty", "tz"),
            P("ax", "ty", "tz"),
            P("ax", "ty", "tz"),
            P(None, "ax", "ty", "tz"),
            P("ax", None, None),
            P("ax", "ty", "tz", None, None),
        ),
        out_specs=(P(None, "ax", "ty", "tz"), P("ax", None, ("ty", "tz"))),
        check_vma=False,
    )
```

```python
import functools
import math

import jax
import jax.numpy as jnp
import numpy as np
from jax import lax
from jax.experimental import pallas as pl
from jax.experimental.pallas import tpu as pltpu
from jax.sharding import PartitionSpec as P

FACE_PLANES = 2
TIME_STEP = 0.6
HALO = 3
EDGE = 8
WEIGHTS = {1: 45.0, 2: -9.0, 3: 1.0}
F32, BF16 = jnp.float32, jnp.bfloat16
VMEM = pl.BlockSpec(memory_space=pltpu.VMEM)
ANY = pl.BlockSpec(memory_space=pl.ANY)
HBM = pl.BlockSpec(memory_space=pltpu.HBM)
ABOVE, BELOW, NONE = 0, 1, 2


def weight_of(offset):
    size = np.abs(offset)
    table = np.zeros(offset.shape, np.float32)
    for s, w in WEIGHTS.items():
        table = np.where(size == s, np.sign(offset) * w, table)
    return table


def tables(nx, ny, nz):
    y, z, layer, x = np.arange(ny), np.arange(nz), np.arange(HALO), np.eye(nx, dtype=np.float32)
    face = np.eye(FACE_PLANES, dtype=np.float32)
    band = weight_of(y[None, :] - y[:, None])
    along_z = weight_of(z[:, None] - z[None, :])

    def from_rows(places, rows):
        w = weight_of(places[None, :] - rows[:, None])
        return np.einsum("xp,yl->xylp", x, w).reshape(nx * EDGE, HALO * nx)

    y_halo = [from_rows(ny + layer, y[ny - EDGE :]), from_rows(layer - HALO, y[:EDGE])]
    y_halo = np.stack(y_halo + [np.zeros((nx * EDGE, HALO * nx))])
    y_face = np.stack(
        [np.kron(face, weight_of(y[None, :] + o - y[:, None])) for o in (ny, -ny)]
        + [np.zeros((FACE_PLANES * ny, FACE_PLANES * ny))]
    )
    z_halo = np.stack([weight_of(z[:, None] + o - z[None, :]) for o in (nz, -nz)] + [np.zeros((nz, nz))])
    twice = lambda m, axis: np.concatenate([m, m], axis=axis)
    columns = lambda m: np.pad(m, [(0, 0)] * (m.ndim - 1) + [(0, -m.shape[-1] % nz)])
    parts = dict(
        ay=np.concatenate(np.split(np.kron(x, band), nx * ny // nz, axis=1)),
        bz=twice(along_z, 0),
        wz=twice(z_halo, 1).reshape(-1, nz),
        py=columns(twice(y_halo, 2)).reshape(-1, nz),
        fy=columns(np.concatenate([twice(np.kron(face, band), 1)[None], twice(y_face, 2)])).reshape(-1, nz),
    )
    places, at = {}, 0
    for name, m in parts.items():
        places[name], at = at, at + m.shape[0]
    return jnp.asarray(np.concatenate(list(parts.values())), BF16), places


class Bands:
    def __init__(self, ref, shape):
        self.ref, (self.nx, self.ny, self.nz) = ref, shape
        self.places = tables(*shape)[1]

    def block(self, name, rows, i=0, width=None):
        at = self.places[name]
        start = at + i * rows if isinstance(i, int) else pl.multiple_of(at + i * rows, 16)
        return self.ref[pl.ds(start, rows), : self.nz if width is None else width]

    def along_y(self):
        rows = self.nx * self.ny
        return jnp.concatenate([self.block("ay", rows, i) for i in range(rows // self.nz)], axis=1)

    def along_z(self):
        return self.block("bz", 2 * self.nz)

    def from_z(self, side):
        return self.block("wz", 2 * self.nz, side)

    def from_y(self, side):
        return self.block("py", self.nx * EDGE, side, 2 * HALO * self.nx)

    def face_y(self, i):
        return self.block("fy", FACE_PLANES * self.ny, i, 2 * FACE_PLANES * self.ny)


def halves(v):
    high = v.astype(BF16)
    return high, (v - high.astype(F32)).astype(BF16)


def stacked(v, axis):
    return jnp.concatenate(halves(v), axis=axis)


def dot(a, b):
    return jnp.dot(a, b, preferred_element_type=F32)


def couple(acc, u, c, d, grad):
    acc = [u * grad[k] if acc is None else acc[k] + u * grad[k] for k in range(5)]
    acc[1 + d] = acc[1 + d] + c * grad[4]
    acc[4] = acc[4] + c * grad[1 + d]
    return acc


def pairs_of(count):
    return count % 2 == 0


def x_sides():
    at, count = lax.axis_index("ax"), lax.axis_size("ax")
    has_lo, has_hi = at > 0, at < count - 1
    if not pairs_of(count):
        return [(False, has_lo), (True, has_hi)]
    even = lax.rem(at, 2) == 0
    return [(even, jnp.where(even, has_hi, has_lo)), (jnp.logical_not(even), jnp.where(even, has_lo, has_hi))]


def sides_of(axis):
    at, count = lax.axis_index(axis), lax.axis_size(axis)
    if count == 2:
        return [at]
    return [jnp.where(at > 0, BELOW, NONE), jnp.where(at < count - 1, ABOVE, NONE)]


def turned(side):
    if isinstance(side, int):
        return (BELOW, ABOVE, NONE)[side]
    return jnp.where(side == NONE, NONE, 1 - side)


def start_of(from_above_next, size):
    if isinstance(from_above_next, bool):
        return size - HALO if from_above_next else 0
    return jnp.where(from_above_next, size - HALO, 0)


def pack_first(adj, vel, c, owner_ref, *refs):
    n_y = len(sides_of("ty"))
    x_msgs, y_msgs, (aux, token, rows, speeds, sems) = refs[:2], refs[2 : 2 + n_y], refs[2 + n_y :]
    nx, ny, nz = adj.shape[1:]
    half = rows.shape[3]
    at = lax.axis_index("ty")
    copies = []

    def copy(src, dst):
        copies.append(pltpu.make_async_copy(src, dst, sems.at[len(copies)]))
        copies[-1].start()

    if n_y == 1:
        tops = [at == 0]
    else:
        tops = [True, False]
    for i, top in enumerate(tops):
        first = (ny - half if top else 0) if isinstance(top, bool) else pl.multiple_of(jnp.where(top, ny - half, 0), 8)
        copy(adj.at[:, :, pl.ds(first, half), :], rows.at[i])
    for ref, (above, _) in zip(x_msgs, x_sides()):
        up = above if pairs_of(lax.axis_size("ax")) else not above
        copy(adj.at[:, pl.ds(start_of(up, nx), HALO)], ref.at[:5])
    copy(vel.at[:, :FACE_PLANES], speeds.at[:3])
    copy(c.at[:FACE_PLANES], speeds.at[3])
    token[...] = jnp.zeros(token.shape, F32)
    blocks = owner_ref.shape[1]
    eye = lax.broadcasted_iota(jnp.int32, (blocks, blocks), 0) == lax.broadcasted_iota(jnp.int32, (blocks, blocks), 1)
    column = jnp.sum(jnp.where(eye, owner_ref[...].astype(F32), 0.0), axis=1, keepdims=True)
    owners = jnp.broadcast_to(column, (blocks, nz)).reshape(FACE_PLANES, ny, nz)
    for one in copies:
        one.wait()
    for d, msgs in enumerate((x_msgs, y_msgs, (aux,))):
        for ref in msgs:
            n = ref.shape[0]
            ref[n - 2, :2] = speeds[d]
            ref[n - 1, :2] = speeds[3]
            ref[n - 2, 2] = owners[0]
            ref[n - 1, 2] = owners[1]
    for i, (ref, top) in enumerate(zip(y_msgs, tops)):

        def put(r, ref=ref, i=i):
            for k in range(5):
                for l in range(HALO):
                    ref[k, l] = rows[i, k, :, r + l, :]

        if isinstance(top, bool):
            put(half - HALO if top else 0)
        else:
            pl.when(top)(functools.partial(put, half - HALO))
            pl.when(jnp.logical_not(top))(functools.partial(put, 0))


def pack_second(v_ref, x_msgs, y_msgs):
    nx, ny = v_ref.shape[1:3]
    for ref, (above, _) in zip(x_msgs, x_sides()):
        up = above if pairs_of(lax.axis_size("ax")) else not above
        ref[...] = v_ref[:, pl.ds(start_of(up, nx), HALO)]

    def put(ref, start):
        for k in range(5):
            for l in range(HALO):
                ref[k, l] = v_ref[k, :, start + l, :]

    if len(y_msgs) == 1:
        at = lax.axis_index("ty")
        pl.when(at == 0)(functools.partial(put, y_msgs[0], ny - HALO))
        pl.when(at != 0)(functools.partial(put, y_msgs[0], 0))
    else:
        put(y_msgs[0], ny - HALO)
        put(y_msgs[1], 0)


def x_difference(v_ref, k, x):
    nx, total = v_ref.shape[1], None
    for s, w in WEIGHTS.items():
        diff = None
        if x + s < nx:
            diff = v_ref[k, x + s]
        if x - s >= 0:
            diff = -v_ref[k, x - s] if diff is None else diff - v_ref[k, x - s]
        if diff is not None:
            diff = diff if w == 1.0 else w * diff
            total = diff if total is None else total + diff
    return total


def own_rate(scale, x, v_ref, adj_ref, vel_ref, c_ref, sponge_ref, source_ref, gy, gz):
    part = scale / 60.0
    c, damp = c_ref[x] * part, sponge_ref[x] * scale
    acc = []
    for k in range(5):
        cur = v_ref[k, x]
        base = cur if adj_ref is None else 0.5 * (adj_ref[k, x] + cur)
        acc.append(base + (scale * source_ref[k, x] - damp * cur))
    gx = [x_difference(v_ref, k, x) for k in range(5)]
    for d, g in enumerate((gx, gy, gz)):
        acc = couple(acc, vel_ref[d, x] * part, c, d, g)
    return acc


def add_x_blocks(scale, out_ref, vel_ref, c_ref, x_blocks):
    nx = out_ref.shape[1]
    for ref, (above, present) in zip(x_blocks, x_sides()):
        keep = jnp.where(present, jnp.where(above, scale / 60.0, -scale / 60.0), 0.0)
        for e in range(HALO):
            x = jnp.where(above, nx - 1 - e, e)
            grad = []
            for k in range(5):
                total = None
                for m in range(HALO - e):
                    w = WEIGHTS[m + 1 + e]
                    term = ref[k, jnp.where(above, m, HALO - 1 - m)]
                    term = term if w == 1.0 else w * term
                    total = term if total is None else total + term
                grad.append(total)
            acc = couple([out_ref[k, x] for k in range(5)], vel_ref[0, x] * keep, c_ref[x] * keep, 0, grad)
            for k in range(5):
                out_ref[k, x] = acc[k]


def own_planes(scale, v_ref, adj_ref, vel_ref, c_ref, sponge_ref, source_ref, table_ref, z_blocks, out_ref, dy, dz):
    nx, ny, nz = v_ref.shape[1:]
    bands = Bands(table_ref, v_ref.shape[1:])
    ay, bz = bands.along_y(), bands.along_z()
    for k in range(5):
        high, low = halves(v_ref[k].reshape(nx * ny, nz))
        dy[k] = (dot(ay, high) + dot(ay, low)).reshape(nx, ny, nz)
        along_z = dot(jnp.concatenate([high, low], axis=1), bz)
        for ref, side in zip(z_blocks, sides_of("tz")):
            along_z = along_z + dot(stacked(ref[k].reshape(nx * ny, nz), 1), bands.from_z(side))
        dz[k] = along_z.reshape(nx, ny, nz)
    for x in range(nx):
        gy, gz = [dy[k, x] for k in range(5)], [dz[k, x] for k in range(5)]
        acc = own_rate(scale, x, v_ref, adj_ref, vel_ref, c_ref, sponge_ref, source_ref, gy, gz)
        for k in range(5):
            out_ref[k, x] = acc[k]


def first_kernel(adj, vel, c, sponge, source, table, _, *refs):
    n_z, refs = len(sides_of("tz")), refs[1:]
    z_blocks, (out_ref, dy, dz) = refs[:n_z], refs[n_z:]
    own_planes(TIME_STEP, adj, None, vel, c, sponge, source, table, z_blocks, out_ref, dy, dz)


def second_kernel(mid, adj, vel, c, sponge, source, table, *refs):
    n_z = len(sides_of("tz"))
    z_blocks, (out_ref, dy, dz) = refs[:n_z], refs[n_z:]
    own_planes(0.5 * TIME_STEP, mid, adj, vel, c, sponge, source, table, z_blocks, out_ref, dy, dz)


def add_y_blocks(scale, out_ref, vel_ref, c_ref, y_blocks, table_ref):
    nx, ny, nz = out_ref.shape[1:]
    bands = Bands(table_ref, out_ref.shape[1:])
    part = scale / 60.0
    for ref, side in zip(y_blocks, sides_of("ty")):
        values = [stacked(ref[k].reshape(HALO * nx, nz), 0) for k in range(5)]
        grads = dot(bands.from_y(side), jnp.concatenate(values, axis=1))
        at = pl.multiple_of(jnp.where(side == ABOVE, ny - EDGE, 0), EDGE)
        for x in range(nx):
            rows = pl.ds(at, EDGE)
            grad = [grads[x * EDGE : (x + 1) * EDGE, k * nz : (k + 1) * nz] for k in range(5)]
            acc = [out_ref[k, x, rows, :] for k in range(5)]
            acc = couple(acc, vel_ref[1, x, rows, :] * part, c_ref[x, rows, :] * part, 1, grad)
            for k in range(5):
                out_ref[k, x, rows, :] = acc[k]


def mid_kernel(part_ref, vel, c, table, *refs):
    n_y = len(sides_of("ty"))
    n_z = len(sides_of("tz"))
    x_blocks, y_blocks, (out_ref, *msgs) = refs[:2], refs[2 : 2 + n_y], refs[2 + n_y + n_z :]
    out_ref[...] = part_ref[...]
    add_y_blocks(TIME_STEP, out_ref, vel, c, y_blocks, table)
    add_x_blocks(TIME_STEP, out_ref, vel, c, x_blocks)
    pack_second(out_ref, msgs[:2], msgs[2:])


def sums_kernel(mid, adj, vel, c, sponge, source, table, owner_ref, *refs):
    n_y, n_z = len(sides_of("ty")), len(sides_of("tz"))
    x_blocks, y_blocks, auxes, sums_ref = refs[:2], refs[2 : 2 + n_y], refs[2 + n_y : 2 + n_y + n_z], refs[-1]
    nx, ny, nz = mid.shape[1:]
    rows = FACE_PLANES * ny
    bands = Bands(table, mid.shape[1:])
    scale = 0.5 * TIME_STEP
    part = scale / 60.0
    flat = lambda v: v.reshape(rows, nz)
    split = [halves(flat(mid[k, :FACE_PLANES])) for k in range(5)]
    tall = jnp.concatenate([jnp.concatenate(pair, axis=0) for pair in split], axis=1)
    wide = jnp.concatenate([jnp.concatenate(pair, axis=1) for pair in split], axis=0)
    along_y = lambda i: [g for g in jnp.split(dot(bands.face_y(i), tall), 5, axis=1)]
    along_z = lambda m: [g for g in jnp.split(dot(wide, m), 5, axis=0)]
    groups, owners = [], []
    gy = [g.reshape(FACE_PLANES, ny, nz) for g in along_y(0)]
    gz = [g.reshape(FACE_PLANES, ny, nz) for g in along_z(bands.along_z())]
    planes = [
        own_rate(scale, p, mid, adj, vel, c, sponge, source, [g[p] for g in gy], [g[p] for g in gz])
        for p in range(FACE_PLANES)
    ]
    groups.append([jnp.concatenate([planes[p][k] for p in range(FACE_PLANES)], axis=0) for k in range(5)])
    eye = lax.broadcasted_iota(jnp.int32, (rows, rows), 0) == lax.broadcasted_iota(jnp.int32, (rows, rows), 1)
    owners.append(jnp.sum(jnp.where(eye, owner_ref[...].astype(F32), 0.0), axis=1, keepdims=True))

    def neighbour(ref, d, keep, grad):
        n = ref.shape[0]
        groups.append(couple(None, flat(ref[n - 2, :2]) * keep, flat(ref[n - 1, :2]) * keep, d, grad))
        owners.append(jnp.concatenate([ref[n - 2, 2], ref[n - 1, 2]], axis=0)[:, :1])

    grad = []
    for k in range(5):
        at_plane = []
        for p in range(FACE_PLANES):
            total = None
            for l in range(p, HALO):
                w = WEIGHTS[HALO + p - l]
                term = mid[k, nx - HALO + l]
                term = term if w == 1.0 else w * term
                total = term if total is None else total + term
            at_plane.append(total)
        grad.append(jnp.concatenate(at_plane, axis=0))
    for ref, (above, present) in zip(x_blocks, x_sides()):
        neighbour(ref, 0, jnp.where(jnp.logical_and(above, present), -part, 0.0), grad)
    for ref, side in zip(y_blocks, sides_of("ty")):
        neighbour(ref, 1, part, along_y(1 + turned(side)))
    for ref, side in zip(auxes, sides_of("tz")):
        neighbour(ref, 2, part, along_z(bands.from_z(turned(side))))

    devices = sums_ref.shape[0]
    each = devices // lax.axis_size("ax")
    total = rows * len(groups)
    place = (lax.broadcasted_iota(jnp.int32, (total, devices), 1) // each).astype(F32)
    choose = (jnp.concatenate(owners, axis=0) == place).astype(F32).astype(BF16)
    choose = jnp.concatenate([choose, choose], axis=0)
    values = [stacked(jnp.concatenate([g[k] for g in groups], axis=0), 0) for k in range(5)]
    sums = lax.dot_general(
        choose, jnp.concatenate(values, axis=1), (((0,), (0,)), ((), ())), preferred_element_type=F32
    )
    sums_ref[:, 5:, :] = jnp.zeros((devices, sums_ref.shape[1] - 5, nz), F32)
    for k in range(5):
        sums_ref[:, k, :] = sums[:, k * nz : (k + 1) * nz]


def final_kernel(part_ref, vel, c, table, *refs):
    n_y = len(sides_of("ty"))
    x_blocks, y_blocks, (out_ref, token, work, sems) = refs[:2], refs[2 : 2 + n_y], refs[2 + n_y :]
    nx = part_ref.shape[1]
    token[...] = jnp.zeros(token.shape, F32)
    scale = 0.5 * TIME_STEP
    work[...] = part_ref[...]
    add_y_blocks(scale, work, vel, c, y_blocks, table)
    inner = pltpu.make_async_copy(work.at[:, HALO : nx - HALO], out_ref.at[:, HALO : nx - HALO], sems.at[0])
    inner.start()
    add_x_blocks(scale, work, vel, c, x_blocks)
    low = pltpu.make_async_copy(work.at[:, :HALO], out_ref.at[:, :HALO], sems.at[1])
    high = pltpu.make_async_copy(work.at[:, nx - HALO :], out_ref.at[:, nx - HALO :], sems.at[2])
    low.start()
    high.start()
    inner.wait()
    low.wait()
    high.wait()


def modes_kernel(scale, sums_ref, basis_ref, _, out_ref):
    share = out_ref.shape[2]
    total = sums_ref[0]
    for i in range(1, sums_ref.shape[0]):
        total = total + sums_ref[i]
    modes = lax.dot_general(
        total, basis_ref[0], (((1,), (0,)), ((), ())), precision=lax.Precision.HIGHEST, preferred_element_type=F32
    )
    mine = lax.axis_index("ty") * lax.axis_size("tz") + lax.axis_index("tz")
    width = modes.shape[1]
    modes = pltpu.roll(modes * scale, lax.rem(width - mine * share, width), 1)
    for k in range(5):
        out_ref[k] = modes[k : k + 1, :share]


def swap_x(first, second):
    count, cores = lax.axis_size("ax"), lax.axis_size("tz")
    if not pairs_of(count):
        return [ring(first, "ax", 1), ring(second, "ax", -1)]
    near = lax.ppermute(first, "ax", [(i, i ^ 1) for i in range(count)])
    pairs = []
    for i in range(count):
        for u in range(cores):
            if i in (0, count - 1):
                pairs.append((i * cores + u, i * cores + (u + 1) % cores))
            else:
                j = i - 1 if i % 2 == 0 else i + 1
                pairs.append((i * cores + u, j * cores + u))
    return [near, lax.ppermute(second, ("ax", "tz"), pairs)]


def ring(v, axis, step):
    count = lax.axis_size(axis)
    return lax.ppermute(v, axis, [(i, (i + step) % count) for i in range(count)])


def from_sides(axis, to_above, to_below):
    if lax.axis_size(axis) == 2:
        return [ring(to_above, axis, 1)]
    return [ring(to_above, axis, 1), ring(to_below, axis, -1)]


def call(kernel, args, outs, scratch=(), away={}, out_away={}, flops=0, grant=12, hint=(20, 10)):
    moved = sum(4 * math.prod(a.shape) for a in (*args, *outs))
    return pl.pallas_call(
        kernel,
        out_shape=list(outs),
        in_specs=[away.get(i, VMEM) for i in range(len(args))],
        out_specs=[out_away.get(i, VMEM) for i in range(len(outs))],
        scratch_shapes=list(scratch),
        cost_estimate=pl.CostEstimate(flops=int(flops * hint[0]), bytes_accessed=int(moved * hint[1]), transcendentals=0),
        compiler_params=pltpu.CompilerParams(vmem_limit_bytes=grant << 20),
    )(*args)


def on_device(adjoint, velocity, sound_speed, sponge, source, mode_basis, block_owner):
    nx, ny, nz = adjoint.shape[1:]
    n_ax, n_ty, n_tz = (lax.axis_size(a) for a in ("ax", "ty", "tz"))
    n_y = 1 if n_ty == 2 else 2
    table, _ = tables(nx, ny, nz)
    shape = lambda *s: jax.ShapeDtypeStruct(s, F32)
    brick = shape(5, nx, ny, nz)
    grads = [pltpu.VMEM((5, nx, ny, nz), F32)] * 2
    work = 5 * nx * ny * nz * 800
    owners = block_owner.reshape(1, FACE_PLANES * ny)
    devices = n_ax * n_ty * n_tz

    *msgs, aux, token = call(
        pack_first,
        [adjoint, velocity, sound_speed, owners],
        [shape(7, HALO, ny, nz)] * 2 + [shape(7, HALO, nx, nz)] * n_y + [shape(2, HALO, ny, nz), shape(8, nz)],
        [pltpu.VMEM((n_y, 5, nx, 8, nz), F32), pltpu.VMEM((4, FACE_PLANES, ny, nz), F32), pltpu.SemaphoreType.DMA((8,))],
        away={0: HBM, 1: HBM, 2: HBM},
        grant=60, flops=10**6,
    )
    z_blocks = from_sides("tz", adjoint, adjoint)
    auxes = from_sides("tz", aux, aux)
    y_first = from_sides("ty", msgs[2], msgs[-1])
    x_first = swap_x(msgs[0], msgs[1])
    fields = [velocity, sound_speed, sponge, source, table]
    (part,) = call(
        first_kernel, [adjoint, *fields, token, owners, *z_blocks], [brick], grads, away={6: ANY}, flops=work, grant=8
    )
    vel, c = velocity, sound_speed
    mid, *msgs = call(
        mid_kernel,
        [part, vel, c, table, *x_first, *y_first, *auxes],
        [brick] + [shape(5, HALO, ny, nz)] * 2 + [shape(5, HALO, nx, nz)] * n_y,
        flops=work // 4,
        grant=8,
    )
    z_blocks = from_sides("tz", mid, mid)
    y_blocks = from_sides("ty", msgs[2], msgs[-1])
    x_blocks = swap_x(msgs[0], msgs[1])
    (sums,) = call(
        sums_kernel,
        [mid, adjoint, vel, c, sponge, source, table, owners, *x_first, *y_first, *auxes],
        [shape(devices, 8, nz)],
        flops=work // 4,
        grant=8,
        hint=(0.02, 0.01),
    )
    sums = lax.all_to_all(sums, ("ax", "ty", "tz"), split_axis=0, concat_axis=0, tiled=True)
    (part,) = call(
        second_kernel, [mid, adjoint, *fields, *z_blocks], [brick], grads, flops=work, grant=8, hint=(0.02, 0.01)
    )
    adjoint_out, token = call(
        final_kernel,
        [part, vel, c, table, *x_blocks, *y_blocks],
        [brick, shape(8, nz)],
        [pltpu.VMEM((5, nx, ny, nz), F32), pltpu.SemaphoreType.DMA((3,))],
        out_away={0: HBM},
        flops=work // 4,
        grant=6,
        hint=(100, 10),
    )
    share = mode_basis.shape[2] // (n_ty * n_tz)
    scale = 1.0 / math.sqrt(FACE_PLANES * ny * n_ty * n_tz)
    (modes,) = call(functools.partial(modes_kernel, scale), [sums, mode_basis, token], [shape(5, 1, share)], grant=2)
    return (adjoint_out, jnp.transpose(modes, (1, 0, 2)))


def solution(mesh):
    return jax.shard_map(
        on_device,
        mesh=mesh,
        in_specs=(
            P(None, "ax", "ty", "tz"),
            P(None, "ax", "ty", "tz"),
            P("ax", "ty", "tz"),
            P("ax", "ty", "tz"),
            P(None, "ax", "ty", "tz"),
            P("ax", None, None),
            P("ax", "ty", "tz", None, None),
        ),
        out_specs=(P(None, "ax", "ty", "tz"), P("ax", None, ("ty", "tz"))),
        check_vma=False,
    )
```

```python
import functools
import math

import jax
import jax.numpy as jnp
import numpy as np
from jax import lax
from jax.experimental import pallas as pl
from jax.experimental.pallas import tpu as pltpu
from jax.sharding import PartitionSpec as P

FACE_PLANES = 2
TIME_STEP = 0.6
HALO = 3
EDGE = 8
WEIGHTS = {1: 45.0, 2: -9.0, 3: 1.0}
F32, BF16 = jnp.float32, jnp.bfloat16
VMEM = pl.BlockSpec(memory_space=pltpu.VMEM)
ANY = pl.BlockSpec(memory_space=pl.ANY)
HBM = pl.BlockSpec(memory_space=pltpu.HBM)
ABOVE, BELOW, NONE = 0, 1, 2


def weight_of(offset):
    size = np.abs(offset)
    table = np.zeros(offset.shape, np.float32)
    for s, w in WEIGHTS.items():
        table = np.where(size == s, np.sign(offset) * w, table)
    return table


def tables(nx, ny, nz):
    y, z, layer, x = np.arange(ny), np.arange(nz), np.arange(HALO), np.eye(nx, dtype=np.float32)
    face = np.eye(FACE_PLANES, dtype=np.float32)
    band = weight_of(y[None, :] - y[:, None])
    along_z = weight_of(z[:, None] - z[None, :])

    def from_rows(places, rows):
        w = weight_of(places[None, :] - rows[:, None])
        return np.einsum("xp,yl->xylp", x, w).reshape(nx * EDGE, HALO * nx)

    y_halo = [from_rows(ny + layer, y[ny - EDGE :]), from_rows(layer - HALO, y[:EDGE])]
    y_halo = np.stack(y_halo + [np.zeros((nx * EDGE, HALO * nx))])
    y_face = np.stack(
        [np.kron(face, weight_of(y[None, :] + o - y[:, None])) for o in (ny, -ny)]
        + [np.zeros((FACE_PLANES * ny, FACE_PLANES * ny))]
    )
    z_halo = np.stack([weight_of(z[:, None] + o - z[None, :]) for o in (nz, -nz)] + [np.zeros((nz, nz))])
    twice = lambda m, axis: np.concatenate([m, m], axis=axis)
    columns = lambda m: np.pad(m, [(0, 0)] * (m.ndim - 1) + [(0, -m.shape[-1] % nz)])
    parts = dict(
        ay=np.concatenate(np.split(np.kron(x, band), nx * ny // nz, axis=1)),
        bz=twice(along_z, 0),
        wz=twice(z_halo, 1).reshape(-1, nz),
        py=columns(twice(y_halo, 2)).reshape(-1, nz),
        fy=columns(np.concatenate([twice(np.kron(face, band), 1)[None], twice(y_face, 2)])).reshape(-1, nz),
    )
    places, at = {}, 0
    for name, m in parts.items():
        places[name], at = at, at + m.shape[0]
    return jnp.asarray(np.concatenate(list(parts.values())), BF16), places


class Bands:
    def __init__(self, ref, shape):
        self.ref, (self.nx, self.ny, self.nz) = ref, shape
        self.places = tables(*shape)[1]

    def block(self, name, rows, i=0, width=None):
        at = self.places[name]
        start = at + i * rows if isinstance(i, int) else pl.multiple_of(at + i * rows, 16)
        return self.ref[pl.ds(start, rows), : self.nz if width is None else width]

    def along_y(self):
        rows = self.nx * self.ny
        return jnp.concatenate([self.block("ay", rows, i) for i in range(rows // self.nz)], axis=1)

    def along_z(self):
        return self.block("bz", 2 * self.nz)

    def from_z(self, side):
        return self.block("wz", 2 * self.nz, side)

    def from_y(self, side):
        return self.block("py", self.nx * EDGE, side, 2 * HALO * self.nx)

    def face_y(self, i):
        return self.block("fy", FACE_PLANES * self.ny, i, 2 * FACE_PLANES * self.ny)


def halves(v):
    high = v.astype(BF16)
    return high, (v - high.astype(F32)).astype(BF16)


def stacked(v, axis):
    return jnp.concatenate(halves(v), axis=axis)


def dot(a, b):
    return jnp.dot(a, b, preferred_element_type=F32)


def couple(acc, u, c, d, grad):
    acc = [u * grad[k] if acc is None else acc[k] + u * grad[k] for k in range(5)]
    acc[1 + d] = acc[1 + d] + c * grad[4]
    acc[4] = acc[4] + c * grad[1 + d]
    return acc


def pairs_of(count):
    return count % 2 == 0


def x_sides():
    at, count = lax.axis_index("ax"), lax.axis_size("ax")
    has_lo, has_hi = at > 0, at < count - 1
    if not pairs_of(count):
        return [(False, has_lo), (True, has_hi)]
    even = lax.rem(at, 2) == 0
    return [(even, jnp.where(even, has_hi, has_lo)), (jnp.logical_not(even), jnp.where(even, has_lo, has_hi))]


def sides_of(axis):
    at, count = lax.axis_index(axis), lax.axis_size(axis)
    if count == 2:
        return [at]
    return [jnp.where(at > 0, BELOW, NONE), jnp.where(at < count - 1, ABOVE, NONE)]


def turned(side):
    if isinstance(side, int):
        return (BELOW, ABOVE, NONE)[side]
    return jnp.where(side == NONE, NONE, 1 - side)


def start_of(from_above_next, size):
    if isinstance(from_above_next, bool):
        return size - HALO if from_above_next else 0
    return jnp.where(from_above_next, size - HALO, 0)


def pack_first(adj, vel, c, owner_ref, *refs):
    n_y = len(sides_of("ty"))
    x_msgs, y_msgs, (aux, token, rows, speeds, names, sems) = refs[:2], refs[2 : 2 + n_y], refs[2 + n_y :]
    nx, ny, nz = adj.shape[1:]
    half = rows.shape[3]
    at = lax.axis_index("ty")
    copies = []

    def copy(src, dst):
        copies.append(pltpu.make_async_copy(src, dst, sems.at[len(copies)]))
        copies[-1].start()

    if n_y == 1:
        tops = [at == 0]
    else:
        tops = [True, False]
    for i, top in enumerate(tops):
        first = (ny - half if top else 0) if isinstance(top, bool) else pl.multiple_of(jnp.where(top, ny - half, 0), 8)
        copy(adj.at[:, :, pl.ds(first, half), :], rows.at[i])
    for ref, (above, _) in zip(x_msgs, x_sides()):
        up = above if pairs_of(lax.axis_size("ax")) else not above
        copy(adj.at[:, pl.ds(start_of(up, nx), HALO)], ref.at[:5])
    copy(vel.at[:, :FACE_PLANES], speeds.at[:3])
    copy(c.at[:FACE_PLANES], speeds.at[3])
    copy(owner_ref, names)
    for one in copies[-3:]:
        one.wait()
    token[...] = jnp.zeros(token.shape, F32)
    blocks = names.shape[1]
    eye = lax.broadcasted_iota(jnp.int32, (blocks, blocks), 0) == lax.broadcasted_iota(jnp.int32, (blocks, blocks), 1)
    column = jnp.sum(jnp.where(eye, names[...].astype(F32), 0.0), axis=1, keepdims=True)
    owners = jnp.broadcast_to(column, (blocks, nz)).reshape(FACE_PLANES, ny, nz)
    for d, msgs in enumerate((x_msgs, y_msgs, (aux,))):
        for ref in msgs:
            n = ref.shape[0]
            ref[n - 2, :2] = speeds[d]
            ref[n - 1, :2] = speeds[3]
            ref[n - 2, 2] = owners[0]
            ref[n - 1, 2] = owners[1]
    for one in copies[:-3]:
        one.wait()
    for i, (ref, top) in enumerate(zip(y_msgs, tops)):

        def put(r, ref=ref, i=i):
            for k in range(5):
                for l in range(HALO):
                    ref[k, l] = rows[i, k, :, r + l, :]

        if isinstance(top, bool):
            put(half - HALO if top else 0)
        else:
            pl.when(top)(functools.partial(put, half - HALO))
            pl.when(jnp.logical_not(top))(functools.partial(put, 0))


def pack_second(v_ref, x_msgs, y_msgs):
    nx, ny = v_ref.shape[1:3]
    for ref, (above, _) in zip(x_msgs, x_sides()):
        up = above if pairs_of(lax.axis_size("ax")) else not above
        ref[...] = v_ref[:, pl.ds(start_of(up, nx), HALO)]

    def put(ref, start):
        for k in range(5):
            for l in range(HALO):
                ref[k, l] = v_ref[k, :, start + l, :]

    if len(y_msgs) == 1:
        at = lax.axis_index("ty")
        pl.when(at == 0)(functools.partial(put, y_msgs[0], ny - HALO))
        pl.when(at != 0)(functools.partial(put, y_msgs[0], 0))
    else:
        put(y_msgs[0], ny - HALO)
        put(y_msgs[1], 0)


def x_difference(v_ref, k, x):
    nx, total = v_ref.shape[1], None
    for s, w in WEIGHTS.items():
        diff = None
        if x + s < nx:
            diff = v_ref[k, x + s]
        if x - s >= 0:
            diff = -v_ref[k, x - s] if diff is None else diff - v_ref[k, x - s]
        if diff is not None:
            diff = diff if w == 1.0 else w * diff
            total = diff if total is None else total + diff
    return total


def own_rate(scale, x, v_ref, adj_ref, vel_ref, c_ref, sponge_ref, source_ref, gy, gz):
    part = scale / 60.0
    c, damp = c_ref[x] * part, sponge_ref[x] * scale
    acc = []
    for k in range(5):
        cur = v_ref[k, x]
        base = cur if adj_ref is None else 0.5 * (adj_ref[k, x] + cur)
        acc.append(base + (scale * source_ref[k, x] - damp * cur))
    gx = [x_difference(v_ref, k, x) for k in range(5)]
    for d, g in enumerate((gx, gy, gz)):
        acc = couple(acc, vel_ref[d, x] * part, c, d, g)
    return acc


def add_x_blocks(scale, out_ref, vel_ref, c_ref, x_blocks):
    nx = out_ref.shape[1]
    for ref, (above, present) in zip(x_blocks, x_sides()):
        keep = jnp.where(present, jnp.where(above, scale / 60.0, -scale / 60.0), 0.0)
        for e in range(HALO):
            x = jnp.where(above, nx - 1 - e, e)
            grad = []
            for k in range(5):
                total = None
                for m in range(HALO - e):
                    w = WEIGHTS[m + 1 + e]
                    term = ref[k, jnp.where(above, m, HALO - 1 - m)]
                    term = term if w == 1.0 else w * term
                    total = term if total is None else total + term
                grad.append(total)
            acc = couple([out_ref[k, x] for k in range(5)], vel_ref[0, x] * keep, c_ref[x] * keep, 0, grad)
            for k in range(5):
                out_ref[k, x] = acc[k]


def own_planes(scale, v_ref, adj_ref, vel_ref, c_ref, sponge_ref, source_ref, table_ref, z_blocks, out_ref, dy, dz):
    nx, ny, nz = v_ref.shape[1:]
    bands = Bands(table_ref, v_ref.shape[1:])
    ay, bz = bands.along_y(), bands.along_z()
    for k in range(5):
        high, low = halves(v_ref[k].reshape(nx * ny, nz))
        dy[k] = (dot(ay, high) + dot(ay, low)).reshape(nx, ny, nz)
        along_z = dot(jnp.concatenate([high, low], axis=1), bz)
        for ref, side in zip(z_blocks, sides_of("tz")):
            along_z = along_z + dot(stacked(ref[k].reshape(nx * ny, nz), 1), bands.from_z(side))
        dz[k] = along_z.reshape(nx, ny, nz)
    for x in range(nx):
        gy, gz = [dy[k, x] for k in range(5)], [dz[k, x] for k in range(5)]
        acc = own_rate(scale, x, v_ref, adj_ref, vel_ref, c_ref, sponge_ref, source_ref, gy, gz)
        for k in range(5):
            out_ref[k, x] = acc[k]


def first_kernel(adj, vel, c, sponge, source, table, _, *refs):
    n_z, refs = len(sides_of("tz")), refs[1:]
    z_blocks, (out_ref, dy, dz) = refs[:n_z], refs[n_z:]
    own_planes(TIME_STEP, adj, None, vel, c, sponge, source, table, z_blocks, out_ref, dy, dz)


def second_kernel(mid, adj, vel, c, sponge, source, table, *refs):
    n_z = len(sides_of("tz"))
    z_blocks, (out_ref, dy, dz) = refs[:n_z], refs[n_z:]
    own_planes(0.5 * TIME_STEP, mid, adj, vel, c, sponge, source, table, z_blocks, out_ref, dy, dz)


def add_y_blocks(scale, out_ref, vel_ref, c_ref, y_blocks, table_ref):
    nx, ny, nz = out_ref.shape[1:]
    bands = Bands(table_ref, out_ref.shape[1:])
    part = scale / 60.0
    for ref, side in zip(y_blocks, sides_of("ty")):
        values = [stacked(ref[k].reshape(HALO * nx, nz), 0) for k in range(5)]
        grads = dot(bands.from_y(side), jnp.concatenate(values, axis=1))
        at = pl.multiple_of(jnp.where(side == ABOVE, ny - EDGE, 0), EDGE)
        for x in range(nx):
            rows = pl.ds(at, EDGE)
            grad = [grads[x * EDGE : (x + 1) * EDGE, k * nz : (k + 1) * nz] for k in range(5)]
            acc = [out_ref[k, x, rows, :] for k in range(5)]
            acc = couple(acc, vel_ref[1, x, rows, :] * part, c_ref[x, rows, :] * part, 1, grad)
            for k in range(5):
                out_ref[k, x, rows, :] = acc[k]


def mid_kernel(part_ref, vel, c, table, *refs):
    n_y = len(sides_of("ty"))
    n_z = len(sides_of("tz"))
    x_blocks, y_blocks, (out_ref, *msgs) = refs[:2], refs[2 : 2 + n_y], refs[2 + n_y + n_z :]
    out_ref[...] = part_ref[...]
    add_y_blocks(TIME_STEP, out_ref, vel, c, y_blocks, table)
    add_x_blocks(TIME_STEP, out_ref, vel, c, x_blocks)
    pack_second(out_ref, msgs[:2], msgs[2:])


def sums_kernel(mid, adj, vel, c, sponge, source, table, owner_ref, *refs):
    n_y, n_z = len(sides_of("ty")), len(sides_of("tz"))
    x_blocks, y_blocks, auxes, sums_ref = refs[:2], refs[2 : 2 + n_y], refs[2 + n_y : 2 + n_y + n_z], refs[-1]
    nx, ny, nz = mid.shape[1:]
    rows = FACE_PLANES * ny
    bands = Bands(table, mid.shape[1:])
    scale = 0.5 * TIME_STEP
    part = scale / 60.0
    flat = lambda v: v.reshape(rows, nz)
    split = [halves(flat(mid[k, :FACE_PLANES])) for k in range(5)]
    tall = jnp.concatenate([jnp.concatenate(pair, axis=0) for pair in split], axis=1)
    wide = jnp.concatenate([jnp.concatenate(pair, axis=1) for pair in split], axis=0)
    along_y = lambda i: [g for g in jnp.split(dot(bands.face_y(i), tall), 5, axis=1)]
    along_z = lambda m: [g for g in jnp.split(dot(wide, m), 5, axis=0)]
    groups, owners = [], []
    gy = [g.reshape(FACE_PLANES, ny, nz) for g in along_y(0)]
    gz = [g.reshape(FACE_PLANES, ny, nz) for g in along_z(bands.along_z())]
    planes = [
        own_rate(scale, p, mid, adj, vel, c, sponge, source, [g[p] for g in gy], [g[p] for g in gz])
        for p in range(FACE_PLANES)
    ]
    groups.append([jnp.concatenate([planes[p][k] for p in range(FACE_PLANES)], axis=0) for k in range(5)])
    eye = lax.broadcasted_iota(jnp.int32, (rows, rows), 0) == lax.broadcasted_iota(jnp.int32, (rows, rows), 1)
    owners.append(jnp.sum(jnp.where(eye, owner_ref[...].astype(F32), 0.0), axis=1, keepdims=True))

    def neighbour(ref, d, keep, grad):
        n = ref.shape[0]
        groups.append(couple(None, flat(ref[n - 2, :2]) * keep, flat(ref[n - 1, :2]) * keep, d, grad))
        owners.append(jnp.concatenate([ref[n - 2, 2], ref[n - 1, 2]], axis=0)[:, :1])

    grad = []
    for k in range(5):
        at_plane = []
        for p in range(FACE_PLANES):
            total = None
            for l in range(p, HALO):
                w = WEIGHTS[HALO + p - l]
                term = mid[k, nx - HALO + l]
                term = term if w == 1.0 else w * term
                total = term if total is None else total + term
            at_plane.append(total)
        grad.append(jnp.concatenate(at_plane, axis=0))
    for ref, (above, present) in zip(x_blocks, x_sides()):
        neighbour(ref, 0, jnp.where(jnp.logical_and(above, present), -part, 0.0), grad)
    for ref, side in zip(y_blocks, sides_of("ty")):
        neighbour(ref, 1, part, along_y(1 + turned(side)))
    for ref, side in zip(auxes, sides_of("tz")):
        neighbour(ref, 2, part, along_z(bands.from_z(turned(side))))

    devices = sums_ref.shape[0]
    each = devices // lax.axis_size("ax")
    total = rows * len(groups)
    place = (lax.broadcasted_iota(jnp.int32, (total, devices), 1) // each).astype(F32)
    choose = (jnp.concatenate(owners, axis=0) == place).astype(F32).astype(BF16)
    choose = jnp.concatenate([choose, choose], axis=0)
    values = [stacked(jnp.concatenate([g[k] for g in groups], axis=0), 0) for k in range(5)]
    sums = lax.dot_general(
        choose, jnp.concatenate(values, axis=1), (((0,), (0,)), ((), ())), preferred_element_type=F32
    )
    sums_ref[:, 5:, :] = jnp.zeros((devices, sums_ref.shape[1] - 5, nz), F32)
    for k in range(5):
        sums_ref[:, k, :] = sums[:, k * nz : (k + 1) * nz]


def final_kernel(part_ref, vel, c, table, *refs):
    n_y = len(sides_of("ty"))
    x_blocks, y_blocks, (out_ref, token, work, sems) = refs[:2], refs[2 : 2 + n_y], refs[2 + n_y :]
    nx = part_ref.shape[1]
    token[...] = jnp.zeros(token.shape, F32)
    scale = 0.5 * TIME_STEP
    work[...] = part_ref[...]
    add_y_blocks(scale, work, vel, c, y_blocks, table)
    inner = pltpu.make_async_copy(work.at[:, HALO : nx - HALO], out_ref.at[:, HALO : nx - HALO], sems.at[0])
    inner.start()
    add_x_blocks(scale, work, vel, c, x_blocks)
    low = pltpu.make_async_copy(work.at[:, :HALO], out_ref.at[:, :HALO], sems.at[1])
    high = pltpu.make_async_copy(work.at[:, nx - HALO :], out_ref.at[:, nx - HALO :], sems.at[2])
    low.start()
    high.start()
    inner.wait()
    low.wait()
    high.wait()


def modes_kernel(scale, sums_ref, basis_ref, _, out_ref):
    share = out_ref.shape[2]
    total = sums_ref[0]
    for i in range(1, sums_ref.shape[0]):
        total = total + sums_ref[i]
    modes = lax.dot_general(
        total, basis_ref[0], (((1,), (0,)), ((), ())), precision=lax.Precision.HIGHEST, preferred_element_type=F32
    )
    mine = lax.axis_index("ty") * lax.axis_size("tz") + lax.axis_index("tz")
    width = modes.shape[1]
    modes = pltpu.roll(modes * scale, lax.rem(width - mine * share, width), 1)
    for k in range(5):
        out_ref[k] = modes[k : k + 1, :share]


def swap_x(first, second):
    count, cores = lax.axis_size("ax"), lax.axis_size("tz")
    if not pairs_of(count):
        return [ring(first, "ax", 1), ring(second, "ax", -1)]
    near = lax.ppermute(first, "ax", [(i, i ^ 1) for i in range(count)])
    pairs = []
    for i in range(count):
        for u in range(cores):
            if i in (0, count - 1):
                pairs.append((i * cores + u, i * cores + (u + 1) % cores))
            else:
                j = i - 1 if i % 2 == 0 else i + 1
                pairs.append((i * cores + u, j * cores + u))
    return [near, lax.ppermute(second, ("ax", "tz"), pairs)]


def ring(v, axis, step):
    count = lax.axis_size(axis)
    return lax.ppermute(v, axis, [(i, (i + step) % count) for i in range(count)])


def from_sides(axis, to_above, to_below):
    if lax.axis_size(axis) == 2:
        return [ring(to_above, axis, 1)]
    return [ring(to_above, axis, 1), ring(to_below, axis, -1)]


def call(kernel, args, outs, scratch=(), away={}, out_away={}, flops=0, grant=12, hint=(20, 10)):
    moved = sum(4 * math.prod(a.shape) for a in (*args, *outs))
    return pl.pallas_call(
        kernel,
        out_shape=list(outs),
        in_specs=[away.get(i, VMEM) for i in range(len(args))],
        out_specs=[out_away.get(i, VMEM) for i in range(len(outs))],
        scratch_shapes=list(scratch),
        cost_estimate=pl.CostEstimate(flops=int(flops * hint[0]), bytes_accessed=int(moved * hint[1]), transcendentals=0),
        compiler_params=pltpu.CompilerParams(vmem_limit_bytes=grant << 20),
    )(*args)


def on_device(adjoint, velocity, sound_speed, sponge, source, mode_basis, block_owner):
    nx, ny, nz = adjoint.shape[1:]
    n_ax, n_ty, n_tz = (lax.axis_size(a) for a in ("ax", "ty", "tz"))
    n_y = 1 if n_ty == 2 else 2
    table, _ = tables(nx, ny, nz)
    shape = lambda *s: jax.ShapeDtypeStruct(s, F32)
    brick = shape(5, nx, ny, nz)
    grads = [pltpu.VMEM((5, nx, ny, nz), F32)] * 2
    work = 5 * nx * ny * nz * 800
    owners = block_owner.reshape(1, FACE_PLANES * ny)
    devices = n_ax * n_ty * n_tz

    *msgs, aux, token = call(
        pack_first,
        [adjoint, velocity, sound_speed, owners],
        [shape(7, HALO, ny, nz)] * 2 + [shape(7, HALO, nx, nz)] * n_y + [shape(2, HALO, ny, nz), shape(8, nz)],
        [pltpu.VMEM((n_y, 5, nx, 8, nz), F32), pltpu.VMEM((4, FACE_PLANES, ny, nz), F32), pltpu.VMEM(owners.shape, jnp.int32), pltpu.SemaphoreType.DMA((8,))],
        away={i: HBM for i in range(4)},
        grant=60, flops=10**6,
    )
    z_blocks = from_sides("tz", adjoint, adjoint)
    auxes = from_sides("tz", aux, aux)
    y_first = from_sides("ty", msgs[2], msgs[-1])
    x_first = swap_x(msgs[0], msgs[1])
    fields = [velocity, sound_speed, sponge, source, table]
    (part,) = call(
        first_kernel, [adjoint, *fields, token, owners, *z_blocks], [brick], grads, away={6: ANY}, flops=work, grant=8
    )
    vel, c = velocity, sound_speed
    mid, *msgs = call(
        mid_kernel,
        [part, vel, c, table, *x_first, *y_first, *auxes],
        [brick] + [shape(5, HALO, ny, nz)] * 2 + [shape(5, HALO, nx, nz)] * n_y,
        flops=work // 4,
        grant=8,
    )
    z_blocks = from_sides("tz", mid, mid)
    y_blocks = from_sides("ty", msgs[2], msgs[-1])
    x_blocks = swap_x(msgs[0], msgs[1])
    (sums,) = call(
        sums_kernel,
        [mid, adjoint, vel, c, sponge, source, table, owners, *x_first, *y_first, *auxes],
        [shape(devices, 8, nz)],
        flops=work // 4,
        grant=8,
    )
    sums = lax.all_to_all(sums, ("ax", "ty", "tz"), split_axis=0, concat_axis=0, tiled=True)
    (part,) = call(
        second_kernel, [mid, adjoint, *fields, *z_blocks], [brick], grads, flops=work, grant=8
    )
    adjoint_out, token = call(
        final_kernel,
        [part, vel, c, table, *x_blocks, *y_blocks],
        [brick, shape(8, nz)],
        [pltpu.VMEM((5, nx, ny, nz), F32), pltpu.SemaphoreType.DMA((3,))],
        out_away={0: HBM},
        flops=work // 4,
        grant=6,
    )
    share = mode_basis.shape[2] // (n_ty * n_tz)
    scale = 1.0 / math.sqrt(FACE_PLANES * ny * n_ty * n_tz)
    (modes,) = call(functools.partial(modes_kernel, scale), [sums, mode_basis, token], [shape(5, 1, share)], grant=2)
    return (adjoint_out, jnp.transpose(modes, (1, 0, 2)))


def solution(mesh):
    return jax.shard_map(
        on_device,
        mesh=mesh,
        in_specs=(
            P(None, "ax", "ty", "tz"),
            P(None, "ax", "ty", "tz"),
            P("ax", "ty", "tz"),
            P("ax", "ty", "tz"),
            P(None, "ax", "ty", "tz"),
            P("ax", None, None),
            P("ax", "ty", "tz", None, None),
        ),
        out_specs=(P(None, "ax", "ty", "tz"), P("ax", None, ("ty", "tz"))),
        check_vma=False,
    )
```

```python
import functools
import math

import jax
import jax.numpy as jnp
import numpy as np
from jax import lax
from jax.experimental import pallas as pl
from jax.experimental.pallas import tpu as pltpu
from jax.sharding import PartitionSpec as P

FACE_PLANES = 2
TIME_STEP = 0.6
HALO = 3
EDGE = 8
WEIGHTS = {1: 45.0, 2: -9.0, 3: 1.0}
F32, BF16 = jnp.float32, jnp.bfloat16
VMEM = pl.BlockSpec(memory_space=pltpu.VMEM)
ANY = pl.BlockSpec(memory_space=pl.ANY)
HBM = pl.BlockSpec(memory_space=pltpu.HBM)
ABOVE, BELOW, NONE = 0, 1, 2


def weight_of(offset):
    size = np.abs(offset)
    table = np.zeros(offset.shape, np.float32)
    for s, w in WEIGHTS.items():
        table = np.where(size == s, np.sign(offset) * w, table)
    return table


def tables(nx, ny, nz):
    sides_y, sides_z = (2 if lax.axis_size(axis) == 2 else 3 for axis in ("ty", "tz"))
    y, z, layer, x = np.arange(ny), np.arange(nz), np.arange(HALO), np.eye(nx, dtype=np.float32)
    face = np.eye(FACE_PLANES, dtype=np.float32)
    band = weight_of(y[None, :] - y[:, None])
    along_z = weight_of(z[:, None] - z[None, :])

    def from_rows(places, rows):
        w = weight_of(places[None, :] - rows[:, None])
        return np.einsum("xp,yl->xylp", x, w).reshape(nx * EDGE, HALO * nx)

    y_halo = [from_rows(ny + layer, y[ny - EDGE :]), from_rows(layer - HALO, y[:EDGE])]
    y_halo = np.stack(y_halo + [np.zeros((nx * EDGE, HALO * nx))])
    y_face = np.stack(
        [np.kron(face, weight_of(y[None, :] + o - y[:, None])) for o in (ny, -ny)]
        + [np.zeros((FACE_PLANES * ny, FACE_PLANES * ny))]
    )
    z_halo = np.stack([weight_of(z[:, None] + o - z[None, :]) for o in (nz, -nz)] + [np.zeros((nz, nz))])
    twice = lambda m, axis: np.concatenate([m, m], axis=axis)
    columns = lambda m: np.pad(m, [(0, 0)] * (m.ndim - 1) + [(0, -m.shape[-1] % nz)])
    parts = dict(
        ay=np.concatenate(np.split(np.kron(x, band), nx * ny // nz, axis=1)),
        bz=twice(along_z, 0),
        wz=twice(z_halo[:sides_z], 1).reshape(-1, nz),
        fy=columns(np.concatenate([twice(np.kron(face, band), 1)[None], twice(y_face[:sides_y], 2)])).reshape(-1, nz),
    )
    places, at = {}, 0
    for name, m in parts.items():
        places[name], at = at, at + m.shape[0]
    edge = columns(twice(y_halo[:sides_y], 2)).reshape(-1, nz)
    return jnp.asarray(np.concatenate(list(parts.values())), BF16), jnp.asarray(edge, BF16), places


class Bands:
    def __init__(self, ref, shape):
        self.ref, (self.nx, self.ny, self.nz) = ref, shape
        self.places = tables(*shape)[2]

    def block(self, name, rows, i=0, width=None):
        at = self.places[name]
        start = at + i * rows if isinstance(i, int) else pl.multiple_of(at + i * rows, 16)
        return self.ref[pl.ds(start, rows), : self.nz if width is None else width]

    def along_y(self):
        rows = self.nx * self.ny
        return jnp.concatenate([self.block("ay", rows, i) for i in range(rows // self.nz)], axis=1)

    def along_z(self):
        return self.block("bz", 2 * self.nz)

    def from_z(self, side):
        return self.block("wz", 2 * self.nz, side)

    def face_y(self, i):
        return self.block("fy", FACE_PLANES * self.ny, i, 2 * FACE_PLANES * self.ny)


def halves(v):
    high = v.astype(BF16)
    return high, (v - high.astype(F32)).astype(BF16)


def stacked(v, axis):
    return jnp.concatenate(halves(v), axis=axis)


def dot(a, b):
    return jnp.dot(a, b, preferred_element_type=F32)


def couple(acc, u, c, d, grad):
    acc = [u * grad[k] if acc is None else acc[k] + u * grad[k] for k in range(5)]
    acc[1 + d] = acc[1 + d] + c * grad[4]
    acc[4] = acc[4] + c * grad[1 + d]
    return acc


def pairs_of(count):
    return count % 2 == 0


def x_sides():
    at, count = lax.axis_index("ax"), lax.axis_size("ax")
    has_lo, has_hi = at > 0, at < count - 1
    if not pairs_of(count):
        return [(False, has_lo), (True, has_hi)]
    even = lax.rem(at, 2) == 0
    return [(even, jnp.where(even, has_hi, has_lo)), (jnp.logical_not(even), jnp.where(even, has_lo, has_hi))]


def sides_of(axis):
    at, count = lax.axis_index(axis), lax.axis_size(axis)
    if count == 2:
        return [at]
    return [jnp.where(at > 0, BELOW, NONE), jnp.where(at < count - 1, ABOVE, NONE)]


def turned(side):
    if isinstance(side, int):
        return (BELOW, ABOVE, NONE)[side]
    return jnp.where(side == NONE, NONE, 1 - side)


def start_of(from_above_next, size):
    if isinstance(from_above_next, bool):
        return size - HALO if from_above_next else 0
    return jnp.where(from_above_next, size - HALO, 0)


def pack_first(adj, vel, c, owner_ref, *refs):
    n_y = len(sides_of("ty"))
    x_msgs, y_msgs, (aux, token, rows, speeds, names, sems) = refs[:2], refs[2 : 2 + n_y], refs[2 + n_y :]
    nx, ny, nz = adj.shape[1:]
    half = rows.shape[3]
    at = lax.axis_index("ty")
    copies = []

    def copy(src, dst):
        copies.append(pltpu.make_async_copy(src, dst, sems.at[len(copies)]))
        copies[-1].start()

    if n_y == 1:
        tops = [at == 0]
    else:
        tops = [True, False]
    for i, top in enumerate(tops):
        first = (ny - half if top else 0) if isinstance(top, bool) else pl.multiple_of(jnp.where(top, ny - half, 0), 8)
        copy(adj.at[:, :, pl.ds(first, half), :], rows.at[i])
    for ref, (above, _) in zip(x_msgs, x_sides()):
        up = above if pairs_of(lax.axis_size("ax")) else not above
        copy(adj.at[:, pl.ds(start_of(up, nx), HALO)], ref.at[:5])
    copy(vel.at[:, :FACE_PLANES], speeds.at[:3])
    copy(c.at[:FACE_PLANES], speeds.at[3])
    copy(owner_ref, names)
    for one in copies[-3:]:
        one.wait()
    token[...] = jnp.zeros(token.shape, F32)
    blocks = names.shape[1]
    eye = lax.broadcasted_iota(jnp.int32, (blocks, blocks), 0) == lax.broadcasted_iota(jnp.int32, (blocks, blocks), 1)
    column = jnp.sum(jnp.where(eye, names[...].astype(F32), 0.0), axis=1, keepdims=True)
    owners = jnp.broadcast_to(column, (blocks, nz)).reshape(FACE_PLANES, ny, nz)
    for d, msgs in enumerate((x_msgs, y_msgs, (aux,))):
        for ref in msgs:
            n = ref.shape[0]
            ref[n - 2, :2] = speeds[d]
            ref[n - 1, :2] = speeds[3]
            ref[n - 2, 2] = owners[0]
            ref[n - 1, 2] = owners[1]
    for one in copies[:-3]:
        one.wait()
    for i, (ref, top) in enumerate(zip(y_msgs, tops)):

        def put(r, ref=ref, i=i):
            for k in range(5):
                for l in range(HALO):
                    ref[k, l] = rows[i, k, :, r + l, :]

        if isinstance(top, bool):
            put(half - HALO if top else 0)
        else:
            pl.when(top)(functools.partial(put, half - HALO))
            pl.when(jnp.logical_not(top))(functools.partial(put, 0))


def pack_second(v_ref, x_msgs, y_msgs):
    nx, ny = v_ref.shape[1:3]
    for ref, (above, _) in zip(x_msgs, x_sides()):
        up = above if pairs_of(lax.axis_size("ax")) else not above
        ref[...] = v_ref[:, pl.ds(start_of(up, nx), HALO)]

    def put(ref, start):
        for k in range(5):
            for l in range(HALO):
                ref[k, l] = v_ref[k, :, start + l, :]

    if len(y_msgs) == 1:
        at = lax.axis_index("ty")
        pl.when(at == 0)(functools.partial(put, y_msgs[0], ny - HALO))
        pl.when(at != 0)(functools.partial(put, y_msgs[0], 0))
    else:
        put(y_msgs[0], ny - HALO)
        put(y_msgs[1], 0)


def x_difference(v_ref, k, x):
    nx, total = v_ref.shape[1], None
    for s, w in WEIGHTS.items():
        diff = None
        if x + s < nx:
            diff = v_ref[k, x + s]
        if x - s >= 0:
            diff = -v_ref[k, x - s] if diff is None else diff - v_ref[k, x - s]
        if diff is not None:
            diff = diff if w == 1.0 else w * diff
            total = diff if total is None else total + diff
    return total


def own_rate(scale, keep, x, v_ref, base, vel_ref, c_ref, sponge_ref, gy, gz):
    part = scale / 60.0
    c, held = c_ref[x] * part, keep - sponge_ref[x] * scale
    acc = [base[k] + held * v_ref[k, x] for k in range(5)]
    gx = [x_difference(v_ref, k, x) for k in range(5)]
    for d, g in enumerate((gx, gy, gz)):
        acc = couple(acc, vel_ref[d, x] * part, c, d, g)
    return acc


def add_x_blocks(scale, out_ref, vel_ref, c_ref, x_blocks):
    nx = out_ref.shape[1]
    for ref, (above, present) in zip(x_blocks, x_sides()):
        keep = jnp.where(present, jnp.where(above, scale / 60.0, -scale / 60.0), 0.0)
        for e in range(HALO):
            x = jnp.where(above, nx - 1 - e, e)
            grad = []
            for k in range(5):
                total = None
                for m in range(HALO - e):
                    w = WEIGHTS[m + 1 + e]
                    term = ref[k, jnp.where(above, m, HALO - 1 - m)]
                    term = term if w == 1.0 else w * term
                    total = term if total is None else total + term
                grad.append(total)
            acc = couple([out_ref[k, x] for k in range(5)], vel_ref[0, x] * keep, c_ref[x] * keep, 0, grad)
            for k in range(5):
                out_ref[k, x] = acc[k]


def own_planes(scale, keep, v_ref, base_of, vel_ref, c_ref, sponge_ref, table_ref, z_blocks, out_ref, dy, dz):
    nx, ny, nz = v_ref.shape[1:]
    bands = Bands(table_ref, v_ref.shape[1:])
    ay, bz = bands.along_y(), bands.along_z()
    for k in range(5):
        high, low = halves(v_ref[k].reshape(nx * ny, nz))
        dy[k] = (dot(ay, high) + dot(ay, low)).reshape(nx, ny, nz)
        along_z = dot(jnp.concatenate([high, low], axis=1), bz)
        for ref, side in zip(z_blocks, sides_of("tz")):
            along_z = along_z + dot(stacked(ref[k].reshape(nx * ny, nz), 1), bands.from_z(side))
        dz[k] = along_z.reshape(nx, ny, nz)
    for x in range(nx):
        gy, gz = [dy[k, x] for k in range(5)], [dz[k, x] for k in range(5)]
        base = [base_of(k, x) for k in range(5)]
        acc = own_rate(scale, keep, x, v_ref, base, vel_ref, c_ref, sponge_ref, gy, gz)
        for k in range(5):
            out_ref[k, x] = acc[k]


def first_kernel(adj, vel, c, sponge, source, table, _, *refs):
    n_z, refs = len(sides_of("tz")), refs[2:]
    z_blocks, (out_ref, base_ref, face_ref, dy, dz) = refs[:n_z], refs[n_z:]
    face_ref[...] = sponge[:FACE_PLANES]

    def base_of(k, x):
        base_ref[k, x] = 0.5 * adj[k, x] + (0.5 * TIME_STEP) * source[k, x]
        return TIME_STEP * source[k, x]

    own_planes(TIME_STEP, 1.0, adj, base_of, vel, c, sponge, table, z_blocks, out_ref, dy, dz)


def second_kernel(mid, base, vel, c, sponge, table, *refs):
    n_z = len(sides_of("tz"))
    z_blocks, (out_ref, dy, dz) = refs[:n_z], refs[n_z:]
    base_of = lambda k, x: base[k, x]
    own_planes(0.5 * TIME_STEP, 0.5, mid, base_of, vel, c, sponge, table, z_blocks, out_ref, dy, dz)


def add_y_blocks(scale, out_ref, vel_ref, c_ref, y_blocks, edge_ref):
    nx, ny, nz = out_ref.shape[1:]
    size = nx * EDGE
    part = scale / 60.0
    for ref, side in zip(y_blocks, sides_of("ty")):
        values = [stacked(ref[k].reshape(HALO * nx, nz), 0) for k in range(5)]
        grads = dot(edge_ref[pl.ds(pl.multiple_of(side * size, 16), size), : 2 * HALO * nx], jnp.concatenate(values, axis=1))
        at = pl.multiple_of(jnp.where(side == ABOVE, ny - EDGE, 0), EDGE)
        for x in range(nx):
            rows = pl.ds(at, EDGE)
            grad = [grads[x * EDGE : (x + 1) * EDGE, k * nz : (k + 1) * nz] for k in range(5)]
            acc = [out_ref[k, x, rows, :] for k in range(5)]
            acc = couple(acc, vel_ref[1, x, rows, :] * part, c_ref[x, rows, :] * part, 1, grad)
            for k in range(5):
                out_ref[k, x, rows, :] = acc[k]


def mid_kernel(part_ref, vel, c, edge, *refs):
    n_y = len(sides_of("ty"))
    n_z = len(sides_of("tz"))
    x_blocks, y_blocks, (out_ref, *msgs) = refs[:2], refs[2 : 2 + n_y], refs[2 + n_y + n_z :]
    out_ref[...] = part_ref[...]
    add_y_blocks(TIME_STEP, out_ref, vel, c, y_blocks, edge)
    add_x_blocks(TIME_STEP, out_ref, vel, c, x_blocks)
    pack_second(out_ref, msgs[:2], msgs[2:])


def sums_kernel(mid, base, vel, c, sponge, table, owner_ref, *refs):
    n_y, n_z = len(sides_of("ty")), len(sides_of("tz"))
    x_blocks, y_blocks, auxes, sums_ref = refs[:2], refs[2 : 2 + n_y], refs[2 + n_y : 2 + n_y + n_z], refs[-1]
    nx, ny, nz = mid.shape[1:]
    rows = FACE_PLANES * ny
    bands = Bands(table, mid.shape[1:])
    scale = 0.5 * TIME_STEP
    part = scale / 60.0
    flat = lambda v: v.reshape(rows, nz)
    split = [halves(flat(mid[k, :FACE_PLANES])) for k in range(5)]
    tall = jnp.concatenate([jnp.concatenate(pair, axis=0) for pair in split], axis=1)
    wide = jnp.concatenate([jnp.concatenate(pair, axis=1) for pair in split], axis=0)
    along_y = lambda i: [g for g in jnp.split(dot(bands.face_y(i), tall), 5, axis=1)]
    along_z = lambda m: [g for g in jnp.split(dot(wide, m), 5, axis=0)]
    groups, owners = [], []
    gy = [g.reshape(FACE_PLANES, ny, nz) for g in along_y(0)]
    gz = [g.reshape(FACE_PLANES, ny, nz) for g in along_z(bands.along_z())]
    planes = [
        own_rate(
            scale, 0.5, p, mid, [base[k, p] for k in range(5)], vel, c, sponge, [g[p] for g in gy], [g[p] for g in gz]
        )
        for p in range(FACE_PLANES)
    ]
    groups.append([jnp.concatenate([planes[p][k] for p in range(FACE_PLANES)], axis=0) for k in range(5)])
    eye = lax.broadcasted_iota(jnp.int32, (rows, rows), 0) == lax.broadcasted_iota(jnp.int32, (rows, rows), 1)
    owners.append(jnp.sum(jnp.where(eye, owner_ref[...].astype(F32), 0.0), axis=1, keepdims=True))

    def neighbour(ref, d, keep, grad):
        n = ref.shape[0]
        groups.append(couple(None, flat(ref[n - 2, :2]) * keep, flat(ref[n - 1, :2]) * keep, d, grad))
        owners.append(jnp.concatenate([ref[n - 2, 2], ref[n - 1, 2]], axis=0)[:, :1])

    grad = []
    for k in range(5):
        at_plane = []
        for p in range(FACE_PLANES):
            total = None
            for l in range(p, HALO):
                w = WEIGHTS[HALO + p - l]
                term = mid[k, nx - HALO + l]
                term = term if w == 1.0 else w * term
                total = term if total is None else total + term
            at_plane.append(total)
        grad.append(jnp.concatenate(at_plane, axis=0))
    for ref, (above, present) in zip(x_blocks, x_sides()):
        neighbour(ref, 0, jnp.where(jnp.logical_and(above, present), -part, 0.0), grad)
    for ref, side in zip(y_blocks, sides_of("ty")):
        neighbour(ref, 1, part, along_y(1 + turned(side)))
    for ref, side in zip(auxes, sides_of("tz")):
        neighbour(ref, 2, part, along_z(bands.from_z(turned(side))))

    devices = sums_ref.shape[0]
    each = devices // lax.axis_size("ax")
    total = rows * len(groups)
    place = (lax.broadcasted_iota(jnp.int32, (total, devices), 1) // each).astype(F32)
    choose = (jnp.concatenate(owners, axis=0) == place).astype(F32).astype(BF16)
    choose = jnp.concatenate([choose, choose], axis=0)
    values = [stacked(jnp.concatenate([g[k] for g in groups], axis=0), 0) for k in range(5)]
    sums = lax.dot_general(
        choose, jnp.concatenate(values, axis=1), (((0,), (0,)), ((), ())), preferred_element_type=F32
    )
    sums_ref[...] = sums.reshape(sums_ref.shape)


def final_kernel(part_ref, vel, c, edge, *refs):
    n_y = len(sides_of("ty"))
    x_blocks, y_blocks, (out_ref, token, work, sems) = refs[:2], refs[2 : 2 + n_y], refs[2 + n_y :]
    nx = part_ref.shape[1]
    token[...] = jnp.zeros(token.shape, F32)
    scale = 0.5 * TIME_STEP
    work[...] = part_ref[...]
    add_y_blocks(scale, work, vel, c, y_blocks, edge)
    inner = pltpu.make_async_copy(work.at[:, HALO : nx - HALO], out_ref.at[:, HALO : nx - HALO], sems.at[0])
    inner.start()
    add_x_blocks(scale, work, vel, c, x_blocks)
    low = pltpu.make_async_copy(work.at[:, :HALO], out_ref.at[:, :HALO], sems.at[1])
    high = pltpu.make_async_copy(work.at[:, nx - HALO :], out_ref.at[:, nx - HALO :], sems.at[2])
    low.start()
    high.start()
    inner.wait()
    low.wait()
    high.wait()


def modes_kernel(scale, sums_ref, basis_ref, _, out_ref):
    share = out_ref.shape[2]
    total = sums_ref[0]
    for i in range(1, sums_ref.shape[0]):
        total = total + sums_ref[i]
    modes = lax.dot_general(
        jnp.concatenate(jnp.split(total, 5, axis=1), axis=0), basis_ref[0], (((1,), (0,)), ((), ())), precision=lax.Precision.HIGHEST, preferred_element_type=F32
    )
    mine = lax.axis_index("ty") * lax.axis_size("tz") + lax.axis_index("tz")
    width = modes.shape[1]
    modes = pltpu.roll(modes * scale, lax.rem(width - mine * share, width), 1)
    for k in range(5):
        out_ref[k] = modes[k : k + 1, :share]


def swap_x(first, second):
    count, cores = lax.axis_size("ax"), lax.axis_size("tz")
    if not pairs_of(count):
        return [ring(first, "ax", 1), ring(second, "ax", -1)]
    near = lax.ppermute(first, "ax", [(i, i ^ 1) for i in range(count)])
    pairs = []
    for i in range(count):
        for u in range(cores):
            if i in (0, count - 1):
                pairs.append((i * cores + u, i * cores + (u + 1) % cores))
            else:
                j = i - 1 if i % 2 == 0 else i + 1
                pairs.append((i * cores + u, j * cores + u))
    return [near, lax.ppermute(second, ("ax", "tz"), pairs)]


def ring(v, axis, step):
    count = lax.axis_size(axis)
    return lax.ppermute(v, axis, [(i, (i + step) % count) for i in range(count)])


def from_sides(axis, to_above, to_below):
    if lax.axis_size(axis) == 2:
        return [ring(to_above, axis, 1)]
    return [ring(to_above, axis, 1), ring(to_below, axis, -1)]


def call(kernel, args, outs, scratch=(), away={}, out_away={}, flops=0, grant=12, hint=(20, 10)):
    moved = sum(4 * math.prod(a.shape) for a in (*args, *outs))
    return pl.pallas_call(
        kernel,
        out_shape=list(outs),
        in_specs=[away.get(i, VMEM) for i in range(len(args))],
        out_specs=[out_away.get(i, VMEM) for i in range(len(outs))],
        scratch_shapes=list(scratch),
        cost_estimate=pl.CostEstimate(flops=int(flops * hint[0]), bytes_accessed=int(moved * hint[1]), transcendentals=0),
        compiler_params=pltpu.CompilerParams(vmem_limit_bytes=grant << 20),
    )(*args)


def on_device(adjoint, velocity, sound_speed, sponge, source, mode_basis, block_owner):
    nx, ny, nz = adjoint.shape[1:]
    n_ax, n_ty, n_tz = (lax.axis_size(a) for a in ("ax", "ty", "tz"))
    n_y = 1 if n_ty == 2 else 2
    table, edge, _ = tables(nx, ny, nz)
    shape = lambda *s: jax.ShapeDtypeStruct(s, F32)
    brick = shape(5, nx, ny, nz)
    grads = [pltpu.VMEM((5, nx, ny, nz), F32)] * 2
    work = 5 * nx * ny * nz * 800
    owners = block_owner.reshape(1, FACE_PLANES * ny)
    devices = n_ax * n_ty * n_tz

    *msgs, aux, token = call(
        pack_first,
        [adjoint, velocity, sound_speed, owners],
        [shape(7, HALO, ny, nz)] * 2 + [shape(7, HALO, nx, nz)] * n_y + [shape(2, HALO, ny, nz), shape(8, nz)],
        [pltpu.VMEM((n_y, 5, nx, 8, nz), F32), pltpu.VMEM((4, FACE_PLANES, ny, nz), F32), pltpu.VMEM(owners.shape, jnp.int32), pltpu.SemaphoreType.DMA((8,))],
        away={i: HBM for i in range(4)},
        grant=60, flops=10**6,
    )
    z_blocks = from_sides("tz", adjoint, adjoint)
    auxes = from_sides("tz", aux, aux)
    y_first = from_sides("ty", msgs[2], msgs[-1])
    x_first = swap_x(msgs[0], msgs[1])
    fields = [velocity, sound_speed, sponge, source, table]
    part, base, face_sponge = call(
        first_kernel, [adjoint, *fields, token, owners, edge, *z_blocks], [brick, brick, shape(FACE_PLANES, ny, nz)], grads, away={6: ANY}, flops=work, grant=8
    )
    vel, c = velocity, sound_speed
    mid, *msgs = call(
        mid_kernel,
        [part, vel, c, edge, *x_first, *y_first, *auxes],
        [brick] + [shape(5, HALO, ny, nz)] * 2 + [shape(5, HALO, nx, nz)] * n_y,
        flops=work // 4,
        grant=8,
    )
    z_blocks = from_sides("tz", mid, mid)
    y_blocks = from_sides("ty", msgs[2], msgs[-1])
    x_blocks = swap_x(msgs[0], msgs[1])
    (sums,) = call(
        sums_kernel,
        [mid, base, vel, c, face_sponge, table, owners, *x_first, *y_first, *auxes],
        [shape(devices, 1, 5 * nz)],
        flops=work // 4,
        grant=8,
    )
    sums = lax.all_to_all(sums, ("ax", "ty", "tz"), split_axis=0, concat_axis=0, tiled=True)
    (part,) = call(
        second_kernel, [mid, base, vel, c, sponge, table, *z_blocks], [brick], grads, flops=work, grant=8
    )
    adjoint_out, token = call(
        final_kernel,
        [part, vel, c, edge, *x_blocks, *y_blocks],
        [brick, shape(8, nz)],
        [pltpu.VMEM((5, nx, ny, nz), F32), pltpu.SemaphoreType.DMA((3,))],
        out_away={0: HBM},
        flops=work // 4,
        grant=6,
    )
    share = mode_basis.shape[2] // (n_ty * n_tz)
    scale = 1.0 / math.sqrt(FACE_PLANES * ny * n_ty * n_tz)
    (modes,) = call(functools.partial(modes_kernel, scale), [sums, mode_basis, token], [shape(5, 1, share)], grant=2)
    return (adjoint_out, jnp.transpose(modes, (1, 0, 2)))


def solution(mesh):
    return jax.shard_map(
        on_device,
        mesh=mesh,
        in_specs=(
            P(None, "ax", "ty", "tz"),
            P(None, "ax", "ty", "tz"),
            P("ax", "ty", "tz"),
            P("ax", "ty", "tz"),
            P(None, "ax", "ty", "tz"),
            P("ax", None, None),
            P("ax", "ty", "tz", None, None),
        ),
        out_specs=(P(None, "ax", "ty", "tz"), P("ax", None, ("ty", "tz"))),
        check_vma=False,
    )
```

```python
import functools
import math

import jax
import jax.numpy as jnp
import numpy as np
from jax import lax
from jax.experimental import pallas as pl
from jax.experimental.pallas import tpu as pltpu
from jax.sharding import PartitionSpec as P

FACE_PLANES = 2
TIME_STEP = 0.6
HALO = 3
EDGE = 8
WEIGHTS = {1: 45.0, 2: -9.0, 3: 1.0}
F32, BF16 = jnp.float32, jnp.bfloat16
VMEM = pl.BlockSpec(memory_space=pltpu.VMEM)
ANY = pl.BlockSpec(memory_space=pl.ANY)
HBM = pl.BlockSpec(memory_space=pltpu.HBM)
ABOVE, BELOW, NONE = 0, 1, 2


def weight_of(offset):
    size = np.abs(offset)
    table = np.zeros(offset.shape, np.float32)
    for s, w in WEIGHTS.items():
        table = np.where(size == s, np.sign(offset) * w, table)
    return table


def tables(nx, ny, nz):
    sides_y, sides_z = (2 if lax.axis_size(axis) == 2 else 3 for axis in ("ty", "tz"))
    y, z, layer, x = np.arange(ny), np.arange(nz), np.arange(HALO), np.eye(nx, dtype=np.float32)
    face = np.eye(FACE_PLANES, dtype=np.float32)
    band = weight_of(y[None, :] - y[:, None])
    along_z = weight_of(z[:, None] - z[None, :])

    def from_rows(places, rows):
        w = weight_of(places[None, :] - rows[:, None])
        return np.einsum("xp,yl->xylp", x, w).reshape(nx * EDGE, HALO * nx)

    y_halo = [from_rows(ny + layer, y[ny - EDGE :]), from_rows(layer - HALO, y[:EDGE])]
    y_halo = np.stack(y_halo + [np.zeros((nx * EDGE, HALO * nx))])
    y_face = np.stack(
        [np.kron(face, weight_of(y[None, :] + o - y[:, None])) for o in (ny, -ny)]
        + [np.zeros((FACE_PLANES * ny, FACE_PLANES * ny))]
    )
    z_halo = np.stack([weight_of(z[:, None] + o - z[None, :]) for o in (nz, -nz)] + [np.zeros((nz, nz))])
    twice = lambda m, axis: np.concatenate([m, m], axis=axis)
    columns = lambda m: np.pad(m, [(0, 0)] * (m.ndim - 1) + [(0, -m.shape[-1] % nz)])
    parts = dict(
        ay=np.concatenate(np.split(np.kron(x, band), nx * ny // nz, axis=1)),
        bz=twice(along_z, 0),
        wz=twice(z_halo[:sides_z], 1).reshape(-1, nz),
        fy=columns(np.concatenate([twice(np.kron(face, band), 1)[None], twice(y_face[:sides_y], 2)])).reshape(-1, nz),
    )
    places, at = {}, 0
    for name, m in parts.items():
        places[name], at = at, at + m.shape[0]
    edge = columns(twice(y_halo[:sides_y], 2)).reshape(-1, nz)
    return jnp.asarray(np.concatenate(list(parts.values())), BF16), jnp.asarray(edge, BF16), places


class Bands:
    def __init__(self, ref, shape, skipped=0):
        self.ref, self.skipped, (self.nx, self.ny, self.nz) = ref, skipped, shape
        self.places = tables(*shape)[2]

    def block(self, name, rows, i=0, width=None):
        at = self.places[name] - self.skipped
        start = at + i * rows if isinstance(i, int) else pl.multiple_of(at + i * rows, 16)
        return self.ref[pl.ds(start, rows), : self.nz if width is None else width]

    def along_y(self):
        rows = self.nx * self.ny
        return jnp.concatenate([self.block("ay", rows, i) for i in range(rows // self.nz)], axis=1)

    def along_z(self):
        return self.block("bz", 2 * self.nz)

    def from_z(self, side):
        return self.block("wz", 2 * self.nz, side)

    def face_y(self, i):
        return self.block("fy", FACE_PLANES * self.ny, i, 2 * FACE_PLANES * self.ny)


def halves(v):
    high = v.astype(BF16)
    return high, (v - high.astype(F32)).astype(BF16)


def stacked(v, axis):
    return jnp.concatenate(halves(v), axis=axis)


def dot(a, b):
    return jnp.dot(a, b, preferred_element_type=F32)


def couple(acc, u, c, d, grad):
    acc = [u * grad[k] if acc is None else acc[k] + u * grad[k] for k in range(5)]
    acc[1 + d] = acc[1 + d] + c * grad[4]
    acc[4] = acc[4] + c * grad[1 + d]
    return acc


def pairs_of(count):
    return count % 2 == 0


def x_sides():
    at, count = lax.axis_index("ax"), lax.axis_size("ax")
    has_lo, has_hi = at > 0, at < count - 1
    if not pairs_of(count):
        return [(False, has_lo), (True, has_hi)]
    even = lax.rem(at, 2) == 0
    return [(even, jnp.where(even, has_hi, has_lo)), (jnp.logical_not(even), jnp.where(even, has_lo, has_hi))]


def sides_of(axis):
    at, count = lax.axis_index(axis), lax.axis_size(axis)
    if count == 2:
        return [at]
    return [jnp.where(at > 0, BELOW, NONE), jnp.where(at < count - 1, ABOVE, NONE)]


def turned(side):
    if isinstance(side, int):
        return (BELOW, ABOVE, NONE)[side]
    return jnp.where(side == NONE, NONE, 1 - side)


def start_of(from_above_next, size):
    if isinstance(from_above_next, bool):
        return size - HALO if from_above_next else 0
    return jnp.where(from_above_next, size - HALO, 0)


def pack_first(adj, vel, c, owner_ref, *refs):
    n_y = len(sides_of("ty"))
    x_msgs, y_msgs, (aux, token, rows, speeds, names, sems) = refs[:2], refs[2 : 2 + n_y], refs[2 + n_y :]
    nx, ny, nz = adj.shape[1:]
    half = rows.shape[3]
    at = lax.axis_index("ty")
    copies = []

    def copy(src, dst):
        copies.append(pltpu.make_async_copy(src, dst, sems.at[len(copies)]))
        copies[-1].start()

    if n_y == 1:
        tops = [at == 0]
    else:
        tops = [True, False]
    for i, top in enumerate(tops):
        first = (ny - half if top else 0) if isinstance(top, bool) else pl.multiple_of(jnp.where(top, ny - half, 0), 8)
        copy(adj.at[:, :, pl.ds(first, half), :], rows.at[i])
    for ref, (above, _) in zip(x_msgs, x_sides()):
        up = above if pairs_of(lax.axis_size("ax")) else not above
        copy(adj.at[:, pl.ds(start_of(up, nx), HALO)], ref.at[:5])
    copy(vel.at[:, :FACE_PLANES], speeds.at[:3])
    copy(c.at[:FACE_PLANES], speeds.at[3])
    copy(owner_ref, names)
    for one in copies[-3:]:
        one.wait()
    token[...] = jnp.zeros(token.shape, F32)
    blocks = names.shape[1]
    eye = lax.broadcasted_iota(jnp.int32, (blocks, blocks), 0) == lax.broadcasted_iota(jnp.int32, (blocks, blocks), 1)
    column = jnp.sum(jnp.where(eye, names[...].astype(F32), 0.0), axis=1, keepdims=True)
    owners = jnp.broadcast_to(column, (blocks, nz)).reshape(FACE_PLANES, ny, nz)
    for d, msgs in enumerate((x_msgs, y_msgs, (aux,))):
        for ref in msgs:
            n = ref.shape[0]
            ref[n - 2, :2] = speeds[d]
            ref[n - 1, :2] = speeds[3]
            ref[n - 2, 2] = owners[0]
            ref[n - 1, 2] = owners[1]
    for one in copies[:-3]:
        one.wait()
    for i, (ref, top) in enumerate(zip(y_msgs, tops)):

        def put(r, ref=ref, i=i):
            for k in range(5):
                for l in range(HALO):
                    ref[k, l] = rows[i, k, :, r + l, :]

        if isinstance(top, bool):
            put(half - HALO if top else 0)
        else:
            pl.when(top)(functools.partial(put, half - HALO))
            pl.when(jnp.logical_not(top))(functools.partial(put, 0))


def pack_second(v_ref, x_msgs, y_msgs):
    nx, ny = v_ref.shape[1:3]
    for ref, (above, _) in zip(x_msgs, x_sides()):
        up = above if pairs_of(lax.axis_size("ax")) else not above
        ref[...] = v_ref[:, pl.ds(start_of(up, nx), HALO)]

    def put(ref, start):
        for k in range(5):
            for l in range(HALO):
                ref[k, l] = v_ref[k, :, start + l, :]

    if len(y_msgs) == 1:
        at = lax.axis_index("ty")
        pl.when(at == 0)(functools.partial(put, y_msgs[0], ny - HALO))
        pl.when(at != 0)(functools.partial(put, y_msgs[0], 0))
    else:
        put(y_msgs[0], ny - HALO)
        put(y_msgs[1], 0)


def x_difference(v_ref, k, x):
    nx, total = v_ref.shape[1], None
    for s, w in WEIGHTS.items():
        diff = None
        if x + s < nx:
            diff = v_ref[k, x + s]
        if x - s >= 0:
            diff = -v_ref[k, x - s] if diff is None else diff - v_ref[k, x - s]
        if diff is not None:
            diff = diff if w == 1.0 else w * diff
            total = diff if total is None else total + diff
    return total


def own_rate(scale, keep, x, v_ref, base, vel_ref, c_ref, sponge_ref, gy, gz):
    part = scale / 60.0
    c, held = c_ref[x] * part, keep - sponge_ref[x] * scale
    acc = [base[k] + held * v_ref[k, x] for k in range(5)]
    gx = [x_difference(v_ref, k, x) for k in range(5)]
    for d, g in enumerate((gx, gy, gz)):
        acc = couple(acc, vel_ref[d, x] * part, c, d, g)
    return acc


def add_x_blocks(scale, out_ref, vel_ref, c_ref, x_blocks):
    nx = out_ref.shape[1]
    for ref, (above, present) in zip(x_blocks, x_sides()):
        keep = jnp.where(present, jnp.where(above, scale / 60.0, -scale / 60.0), 0.0)
        for e in range(HALO):
            x = jnp.where(above, nx - 1 - e, e)
            grad = []
            for k in range(5):
                total = None
                for m in range(HALO - e):
                    w = WEIGHTS[m + 1 + e]
                    term = ref[k, jnp.where(above, m, HALO - 1 - m)]
                    term = term if w == 1.0 else w * term
                    total = term if total is None else total + term
                grad.append(total)
            acc = couple([out_ref[k, x] for k in range(5)], vel_ref[0, x] * keep, c_ref[x] * keep, 0, grad)
            for k in range(5):
                out_ref[k, x] = acc[k]


def own_planes(scale, keep, v_ref, base_of, vel_ref, c_ref, sponge_ref, table_ref, z_blocks, out_ref, dy, dz):
    nx, ny, nz = v_ref.shape[1:]
    bands = Bands(table_ref, v_ref.shape[1:])
    ay, bz = bands.along_y(), bands.along_z()
    for k in range(5):
        high, low = halves(v_ref[k].reshape(nx * ny, nz))
        dy[k] = (dot(ay, high) + dot(ay, low)).reshape(nx, ny, nz)
        along_z = dot(jnp.concatenate([high, low], axis=1), bz)
        for ref, side in zip(z_blocks, sides_of("tz")):
            along_z = along_z + dot(stacked(ref[k].reshape(nx * ny, nz), 1), bands.from_z(side))
        dz[k] = along_z.reshape(nx, ny, nz)
    for x in range(nx):
        gy, gz = [dy[k, x] for k in range(5)], [dz[k, x] for k in range(5)]
        base = [base_of(k, x) for k in range(5)]
        acc = own_rate(scale, keep, x, v_ref, base, vel_ref, c_ref, sponge_ref, gy, gz)
        for k in range(5):
            out_ref[k, x] = acc[k]


def first_kernel(adj, vel, c, sponge, source, table, _, *refs):
    n_z, refs = len(sides_of("tz")), refs[2:]
    z_blocks, (out_ref, base_ref, face_ref, bands_ref, dy, dz) = refs[:n_z], refs[n_z:]
    face_ref[...] = sponge[:FACE_PLANES]
    bands_ref[...] = table[table.shape[0] - bands_ref.shape[0] :]

    def base_of(k, x):
        base_ref[k, x] = 0.5 * adj[k, x] + (0.5 * TIME_STEP) * source[k, x]
        return TIME_STEP * source[k, x]

    own_planes(TIME_STEP, 1.0, adj, base_of, vel, c, sponge, table, z_blocks, out_ref, dy, dz)


def second_kernel(mid, base, vel, c, sponge, table, *refs):
    n_z = len(sides_of("tz"))
    z_blocks, (out_ref, dy, dz) = refs[:n_z], refs[n_z:]
    base_of = lambda k, x: base[k, x]
    own_planes(0.5 * TIME_STEP, 0.5, mid, base_of, vel, c, sponge, table, z_blocks, out_ref, dy, dz)


def add_y_blocks(scale, out_ref, vel_ref, c_ref, y_blocks, edge_ref):
    nx, ny, nz = out_ref.shape[1:]
    size = nx * EDGE
    part = scale / 60.0
    for ref, side in zip(y_blocks, sides_of("ty")):
        values = [stacked(ref[k].reshape(HALO * nx, nz), 0) for k in range(5)]
        grads = dot(edge_ref[pl.ds(pl.multiple_of(side * size, 16), size), : 2 * HALO * nx], jnp.concatenate(values, axis=1))
        at = pl.multiple_of(jnp.where(side == ABOVE, ny - EDGE, 0), EDGE)
        for x in range(nx):
            rows = pl.ds(at, EDGE)
            grad = [grads[x * EDGE : (x + 1) * EDGE, k * nz : (k + 1) * nz] for k in range(5)]
            acc = [out_ref[k, x, rows, :] for k in range(5)]
            acc = couple(acc, vel_ref[1, x, rows, :] * part, c_ref[x, rows, :] * part, 1, grad)
            for k in range(5):
                out_ref[k, x, rows, :] = acc[k]


def mid_kernel(part_ref, vel, c, edge, *refs):
    n_y = len(sides_of("ty"))
    n_z = len(sides_of("tz"))
    x_blocks, y_blocks, (out_ref, *msgs) = refs[:2], refs[2 : 2 + n_y], refs[2 + n_y + n_z :]
    out_ref[...] = part_ref[...]
    add_y_blocks(TIME_STEP, out_ref, vel, c, y_blocks, edge)
    add_x_blocks(TIME_STEP, out_ref, vel, c, x_blocks)
    pack_second(out_ref, msgs[:2], msgs[2:])


def sums_kernel(mid, base, vel, c, sponge, table, owner_ref, *refs):
    n_y, n_z = len(sides_of("ty")), len(sides_of("tz"))
    x_blocks, y_blocks, auxes, sums_ref = refs[:2], refs[2 : 2 + n_y], refs[2 + n_y : 2 + n_y + n_z], refs[-1]
    nx, ny, nz = mid.shape[1:]
    rows = FACE_PLANES * ny
    bands = Bands(table, mid.shape[1:], tables(*mid.shape[1:])[2]["bz"])
    scale = 0.5 * TIME_STEP
    part = scale / 60.0
    flat = lambda v: v.reshape(rows, nz)
    split = [halves(flat(mid[k, :FACE_PLANES])) for k in range(5)]
    tall = jnp.concatenate([jnp.concatenate(pair, axis=0) for pair in split], axis=1)
    wide = jnp.concatenate([jnp.concatenate(pair, axis=1) for pair in split], axis=0)
    along_y = lambda i: [g for g in jnp.split(dot(bands.face_y(i), tall), 5, axis=1)]
    along_z = lambda m: [g for g in jnp.split(dot(wide, m), 5, axis=0)]
    groups, owners = [], []
    gy = [g.reshape(FACE_PLANES, ny, nz) for g in along_y(0)]
    gz = [g.reshape(FACE_PLANES, ny, nz) for g in along_z(bands.along_z())]
    planes = [
        own_rate(
            scale, 0.5, p, mid, [base[k, p] for k in range(5)], vel, c, sponge, [g[p] for g in gy], [g[p] for g in gz]
        )
        for p in range(FACE_PLANES)
    ]
    groups.append([jnp.concatenate([planes[p][k] for p in range(FACE_PLANES)], axis=0) for k in range(5)])
    eye = lax.broadcasted_iota(jnp.int32, (rows, rows), 0) == lax.broadcasted_iota(jnp.int32, (rows, rows), 1)
    owners.append(jnp.sum(jnp.where(eye, owner_ref[...].astype(F32), 0.0), axis=1, keepdims=True))

    def neighbour(ref, d, keep, grad):
        n = ref.shape[0]
        groups.append(couple(None, flat(ref[n - 2, :2]) * keep, flat(ref[n - 1, :2]) * keep, d, grad))
        owners.append(jnp.concatenate([ref[n - 2, 2], ref[n - 1, 2]], axis=0)[:, :1])

    grad = []
    for k in range(5):
        at_plane = []
        for p in range(FACE_PLANES):
            total = None
            for l in range(p, HALO):
                w = WEIGHTS[HALO + p - l]
                term = mid[k, nx - HALO + l]
                term = term if w == 1.0 else w * term
                total = term if total is None else total + term
            at_plane.append(total)
        grad.append(jnp.concatenate(at_plane, axis=0))
    for ref, (above, present) in zip(x_blocks, x_sides()):
        neighbour(ref, 0, jnp.where(jnp.logical_and(above, present), -part, 0.0), grad)
    for ref, side in zip(y_blocks, sides_of("ty")):
        neighbour(ref, 1, part, along_y(1 + turned(side)))
    for ref, side in zip(auxes, sides_of("tz")):
        neighbour(ref, 2, part, along_z(bands.from_z(turned(side))))

    devices = sums_ref.shape[0]
    each = devices // lax.axis_size("ax")
    total = rows * len(groups)
    place = (lax.broadcasted_iota(jnp.int32, (total, devices), 1) // each).astype(F32)
    choose = (jnp.concatenate(owners, axis=0) == place).astype(F32).astype(BF16)
    choose = jnp.concatenate([choose, choose], axis=0)
    values = [stacked(jnp.concatenate([g[k] for g in groups], axis=0), 0) for k in range(5)]
    sums = lax.dot_general(
        choose, jnp.concatenate(values, axis=1), (((0,), (0,)), ((), ())), preferred_element_type=F32
    )
    sums_ref[...] = sums.reshape(sums_ref.shape)


def final_kernel(part_ref, vel, c, edge, *refs):
    n_y = len(sides_of("ty"))
    x_blocks, y_blocks, (out_ref, token, work, sems) = refs[:2], refs[2 : 2 + n_y], refs[2 + n_y :]
    nx = part_ref.shape[1]
    token[...] = jnp.zeros(token.shape, F32)
    scale = 0.5 * TIME_STEP
    work[...] = part_ref[...]
    add_y_blocks(scale, work, vel, c, y_blocks, edge)
    inner = pltpu.make_async_copy(work.at[:, HALO : nx - HALO], out_ref.at[:, HALO : nx - HALO], sems.at[0])
    inner.start()
    add_x_blocks(scale, work, vel, c, x_blocks)
    low = pltpu.make_async_copy(work.at[:, :HALO], out_ref.at[:, :HALO], sems.at[1])
    high = pltpu.make_async_copy(work.at[:, nx - HALO :], out_ref.at[:, nx - HALO :], sems.at[2])
    low.start()
    high.start()
    inner.wait()
    low.wait()
    high.wait()


def modes_kernel(scale, sums_ref, basis_ref, _, out_ref):
    share = out_ref.shape[2]
    total = sums_ref[0]
    for i in range(1, sums_ref.shape[0]):
        total = total + sums_ref[i]
    modes = lax.dot_general(
        jnp.concatenate(jnp.split(total, 5, axis=1), axis=0), basis_ref[0], (((1,), (0,)), ((), ())), precision=lax.Precision.HIGHEST, preferred_element_type=F32
    )
    mine = lax.axis_index("ty") * lax.axis_size("tz") + lax.axis_index("tz")
    width = modes.shape[1]
    modes = pltpu.roll(modes * scale, lax.rem(width - mine * share, width), 1)
    for k in range(5):
        out_ref[k] = modes[k : k + 1, :share]


def swap_x(first, second):
    count, cores = lax.axis_size("ax"), lax.axis_size("tz")
    if not pairs_of(count):
        return [ring(first, "ax", 1), ring(second, "ax", -1)]
    near = lax.ppermute(first, "ax", [(i, i ^ 1) for i in range(count)])
    pairs = []
    for i in range(count):
        for u in range(cores):
            if i in (0, count - 1):
                pairs.append((i * cores + u, i * cores + (u + 1) % cores))
            else:
                j = i - 1 if i % 2 == 0 else i + 1
                pairs.append((i * cores + u, j * cores + u))
    return [near, lax.ppermute(second, ("ax", "tz"), pairs)]


def ring(v, axis, step):
    count = lax.axis_size(axis)
    return lax.ppermute(v, axis, [(i, (i + step) % count) for i in range(count)])


def from_sides(axis, to_above, to_below):
    if lax.axis_size(axis) == 2:
        return [ring(to_above, axis, 1)]
    return [ring(to_above, axis, 1), ring(to_below, axis, -1)]


def call(kernel, args, outs, scratch=(), away={}, out_away={}, flops=0, grant=12, hint=(20, 10)):
    moved = sum(4 * math.prod(a.shape) for a in (*args, *outs))
    return pl.pallas_call(
        kernel,
        out_shape=list(outs),
        in_specs=[away.get(i, VMEM) for i in range(len(args))],
        out_specs=[out_away.get(i, VMEM) for i in range(len(outs))],
        scratch_shapes=list(scratch),
        cost_estimate=pl.CostEstimate(flops=int(flops * hint[0]), bytes_accessed=int(moved * hint[1]), transcendentals=0),
        compiler_params=pltpu.CompilerParams(vmem_limit_bytes=grant << 20),
    )(*args)


def on_device(adjoint, velocity, sound_speed, sponge, source, mode_basis, block_owner):
    nx, ny, nz = adjoint.shape[1:]
    n_ax, n_ty, n_tz = (lax.axis_size(a) for a in ("ax", "ty", "tz"))
    n_y = 1 if n_ty == 2 else 2
    table, edge, places = tables(nx, ny, nz)
    shape = lambda *s: jax.ShapeDtypeStruct(s, F32)
    brick = shape(5, nx, ny, nz)
    grads = [pltpu.VMEM((5, nx, ny, nz), F32)] * 2
    work = 5 * nx * ny * nz * 800
    owners = block_owner.reshape(1, FACE_PLANES * ny)
    devices = n_ax * n_ty * n_tz

    *msgs, aux, token = call(
        pack_first,
        [adjoint, velocity, sound_speed, owners],
        [shape(7, HALO, ny, nz)] * 2 + [shape(7, HALO, nx, nz)] * n_y + [shape(2, HALO, ny, nz), shape(8, nz)],
        [pltpu.VMEM((n_y, 5, nx, 8, nz), F32), pltpu.VMEM((4, FACE_PLANES, ny, nz), F32), pltpu.VMEM(owners.shape, jnp.int32), pltpu.SemaphoreType.DMA((8,))],
        away={i: HBM for i in range(4)},
        grant=60, flops=10**6,
    )
    z_blocks = from_sides("tz", adjoint, adjoint)
    auxes = from_sides("tz", aux, aux)
    y_first = from_sides("ty", msgs[2], msgs[-1])
    x_first = swap_x(msgs[0], msgs[1])
    fields = [velocity, sound_speed, sponge, source, table]
    part, base, face_sponge, face_table = call(
        first_kernel, [adjoint, *fields, token, owners, edge, *z_blocks], [brick, brick, shape(FACE_PLANES, ny, nz), jax.ShapeDtypeStruct((table.shape[0] - places["bz"], nz), BF16)], grads, away={6: ANY}, flops=work, grant=8
    )
    vel, c = velocity, sound_speed
    mid, *msgs = call(
        mid_kernel,
        [part, vel, c, edge, *x_first, *y_first, *auxes],
        [brick] + [shape(5, HALO, ny, nz)] * 2 + [shape(5, HALO, nx, nz)] * n_y,
        flops=work // 4,
        grant=8,
    )
    z_blocks = from_sides("tz", mid, mid)
    y_blocks = from_sides("ty", msgs[2], msgs[-1])
    x_blocks = swap_x(msgs[0], msgs[1])
    (sums,) = call(
        sums_kernel,
        [mid, base, vel, c, face_sponge, face_table, owners, *x_first, *y_first, *auxes],
        [shape(devices, 1, 5 * nz)],
        flops=work // 4,
        grant=8,
    )
    sums = lax.all_to_all(sums, ("ax", "ty", "tz"), split_axis=0, concat_axis=0, tiled=True)
    (part,) = call(
        second_kernel, [mid, base, vel, c, sponge, table, *z_blocks], [brick], grads, flops=work, grant=8
    )
    adjoint_out, token = call(
        final_kernel,
        [part, vel, c, edge, *x_blocks, *y_blocks],
        [brick, shape(8, nz)],
        [pltpu.VMEM((5, nx, ny, nz), F32), pltpu.SemaphoreType.DMA((3,))],
        out_away={0: HBM},
        flops=work // 4,
        grant=6,
    )
    share = mode_basis.shape[2] // (n_ty * n_tz)
    scale = 1.0 / math.sqrt(FACE_PLANES * ny * n_ty * n_tz)
    (modes,) = call(functools.partial(modes_kernel, scale), [sums, mode_basis, token], [shape(5, 1, share)], grant=2)
    return (adjoint_out, jnp.transpose(modes, (1, 0, 2)))


def solution(mesh):
    return jax.shard_map(
        on_device,
        mesh=mesh,
        in_specs=(
            P(None, "ax", "ty", "tz"),
            P(None, "ax", "ty", "tz"),
            P("ax", "ty", "tz"),
            P("ax", "ty", "tz"),
            P(None, "ax", "ty", "tz"),
            P("ax", None, None),
            P("ax", "ty", "tz", None, None),
        ),
        out_specs=(P(None, "ax", "ty", "tz"), P("ax", None, ("ty", "tz"))),
        check_vma=False,
    )
```

```python
import functools
import math

import jax
import jax.numpy as jnp
import numpy as np
from jax import lax
from jax.experimental import pallas as pl
from jax.experimental.pallas import tpu as pltpu
from jax.sharding import PartitionSpec as P

FACE_PLANES = 2
TIME_STEP = 0.6
HALO = 3
EDGE = 8
WEIGHTS = {1: 45.0, 2: -9.0, 3: 1.0}
F32, BF16 = jnp.float32, jnp.bfloat16
VMEM = pl.BlockSpec(memory_space=pltpu.VMEM)
ANY = pl.BlockSpec(memory_space=pl.ANY)
HBM = pl.BlockSpec(memory_space=pltpu.HBM)
ABOVE, BELOW, NONE = 0, 1, 2


def weight_of(offset):
    size = np.abs(offset)
    table = np.zeros(offset.shape, np.float32)
    for s, w in WEIGHTS.items():
        table = np.where(size == s, np.sign(offset) * w, table)
    return table


def tables(nx, ny, nz):
    sides_y, sides_z = (2 if lax.axis_size(axis) == 2 else 3 for axis in ("ty", "tz"))
    y, z, layer, x = np.arange(ny), np.arange(nz), np.arange(HALO), np.eye(nx, dtype=np.float32)
    face = np.eye(FACE_PLANES, dtype=np.float32)
    band = weight_of(y[None, :] - y[:, None])
    along_z = weight_of(z[:, None] - z[None, :])

    def from_rows(places, rows):
        w = weight_of(places[None, :] - rows[:, None])
        return np.einsum("xp,yl->xylp", x, w).reshape(nx * EDGE, HALO * nx)

    y_halo = [from_rows(ny + layer, y[ny - EDGE :]), from_rows(layer - HALO, y[:EDGE])]
    y_halo = np.stack(y_halo + [np.zeros((nx * EDGE, HALO * nx))])
    y_face = np.stack(
        [np.kron(face, weight_of(y[None, :] + o - y[:, None])) for o in (ny, -ny)]
        + [np.zeros((FACE_PLANES * ny, FACE_PLANES * ny))]
    )
    z_halo = np.stack([weight_of(z[:, None] + o - z[None, :]) for o in (nz, -nz)] + [np.zeros((nz, nz))])
    twice = lambda m, axis: np.concatenate([m, m], axis=axis)
    columns = lambda m: np.pad(m, [(0, 0)] * (m.ndim - 1) + [(0, -m.shape[-1] % nz)])
    parts = dict(
        ay=np.concatenate(np.split(np.kron(x, band), nx * ny // nz, axis=1)),
        bz=twice(along_z, 0),
        wz=twice(z_halo[:sides_z], 1).reshape(-1, nz),
        fy=columns(np.concatenate([twice(np.kron(face, band), 1)[None], twice(y_face[:sides_y], 2)])).reshape(-1, nz),
    )
    places, at = {}, 0
    for name, m in parts.items():
        places[name], at = at, at + m.shape[0]
    edge = columns(twice(y_halo[:sides_y], 2)).reshape(-1, nz)
    return jnp.asarray(np.concatenate(list(parts.values())), BF16), jnp.asarray(edge, BF16), places


class Bands:
    def __init__(self, ref, shape, skipped=0):
        self.ref, self.skipped, (self.nx, self.ny, self.nz) = ref, skipped, shape
        self.places = tables(*shape)[2]

    def block(self, name, rows, i=0, width=None):
        at = self.places[name] - self.skipped
        start = at + i * rows if isinstance(i, int) else pl.multiple_of(at + i * rows, 16)
        return self.ref[pl.ds(start, rows), : self.nz if width is None else width]

    def along_y(self):
        rows = self.nx * self.ny
        return jnp.concatenate([self.block("ay", rows, i) for i in range(rows // self.nz)], axis=1)

    def along_z(self):
        return self.block("bz", 2 * self.nz)

    def from_z(self, side):
        return self.block("wz", 2 * self.nz, side)

    def face_y(self, i):
        return self.block("fy", FACE_PLANES * self.ny, i, 2 * FACE_PLANES * self.ny)


def halves(v):
    high = v.astype(BF16)
    return high, (v - high.astype(F32)).astype(BF16)


def stacked(v, axis):
    return jnp.concatenate(halves(v), axis=axis)


def dot(a, b):
    return jnp.dot(a, b, preferred_element_type=F32)


def couple(acc, u, c, d, grad):
    acc = [u * grad[k] if acc is None else acc[k] + u * grad[k] for k in range(5)]
    acc[1 + d] = acc[1 + d] + c * grad[4]
    acc[4] = acc[4] + c * grad[1 + d]
    return acc


def pairs_of(count):
    return count % 2 == 0


def x_sides():
    at, count = lax.axis_index("ax"), lax.axis_size("ax")
    has_lo, has_hi = at > 0, at < count - 1
    if not pairs_of(count):
        return [(False, has_lo), (True, has_hi)]
    even = lax.rem(at, 2) == 0
    return [(even, jnp.where(even, has_hi, has_lo)), (jnp.logical_not(even), jnp.where(even, has_lo, has_hi))]


def sides_of(axis):
    at, count = lax.axis_index(axis), lax.axis_size(axis)
    if count == 2:
        return [at]
    return [jnp.where(at > 0, BELOW, NONE), jnp.where(at < count - 1, ABOVE, NONE)]


def turned(side):
    if isinstance(side, int):
        return (BELOW, ABOVE, NONE)[side]
    return jnp.where(side == NONE, NONE, 1 - side)


def start_of(from_above_next, size):
    if isinstance(from_above_next, bool):
        return size - HALO if from_above_next else 0
    return jnp.where(from_above_next, size - HALO, 0)


def pack_first(adj, vel, c, owner_ref, *refs):
    n_y = len(sides_of("ty"))
    x_msgs, y_msgs, (aux, token, rows, speeds, names, sems) = refs[:2], refs[2 : 2 + n_y], refs[2 + n_y :]
    nx, ny, nz = adj.shape[1:]
    half = rows.shape[3]
    at = lax.axis_index("ty")
    copies = []

    def copy(src, dst):
        copies.append(pltpu.make_async_copy(src, dst, sems.at[len(copies)]))
        copies[-1].start()

    if n_y == 1:
        tops = [at == 0]
    else:
        tops = [True, False]
    for i, top in enumerate(tops):
        first = (ny - half if top else 0) if isinstance(top, bool) else pl.multiple_of(jnp.where(top, ny - half, 0), 8)
        copy(adj.at[:, :, pl.ds(first, half), :], rows.at[i])
    for ref, (above, _) in zip(x_msgs, x_sides()):
        up = above if pairs_of(lax.axis_size("ax")) else not above
        copy(adj.at[:, pl.ds(start_of(up, nx), HALO)], ref.at[:5])
    copy(vel.at[:, :FACE_PLANES], speeds.at[:3])
    copy(c.at[:FACE_PLANES], speeds.at[3])
    copy(owner_ref, names)
    for one in copies[-3:]:
        one.wait()
    token[...] = jnp.zeros(token.shape, F32)
    blocks = names.shape[1]
    eye = lax.broadcasted_iota(jnp.int32, (blocks, blocks), 0) == lax.broadcasted_iota(jnp.int32, (blocks, blocks), 1)
    column = jnp.sum(jnp.where(eye, names[...].astype(F32), 0.0), axis=1, keepdims=True)
    owners = jnp.broadcast_to(column, (blocks, nz)).reshape(FACE_PLANES, ny, nz)
    for d, msgs in enumerate((x_msgs, y_msgs, (aux,))):
        for ref in msgs:
            n = ref.shape[0]
            ref[n - 2, :2] = speeds[d]
            ref[n - 1, :2] = speeds[3]
            ref[n - 2, 2] = owners[0]
            ref[n - 1, 2] = owners[1]
    for one in copies[:-3]:
        one.wait()
    for i, (ref, top) in enumerate(zip(y_msgs, tops)):

        def put(r, ref=ref, i=i):
            for k in range(5):
                for l in range(HALO):
                    ref[k, l] = rows[i, k, :, r + l, :]

        if isinstance(top, bool):
            put(half - HALO if top else 0)
        else:
            pl.when(top)(functools.partial(put, half - HALO))
            pl.when(jnp.logical_not(top))(functools.partial(put, 0))


def pack_second(v_ref, x_msgs, y_msgs):
    nx, ny = v_ref.shape[1:3]
    for ref, (above, _) in zip(x_msgs, x_sides()):
        up = above if pairs_of(lax.axis_size("ax")) else not above
        ref[...] = v_ref[:, pl.ds(start_of(up, nx), HALO)]

    def put(ref, start):
        for k in range(5):
            for l in range(HALO):
                ref[k, l] = v_ref[k, :, start + l, :]

    if len(y_msgs) == 1:
        at = lax.axis_index("ty")
        pl.when(at == 0)(functools.partial(put, y_msgs[0], ny - HALO))
        pl.when(at != 0)(functools.partial(put, y_msgs[0], 0))
    else:
        put(y_msgs[0], ny - HALO)
        put(y_msgs[1], 0)


def x_difference(v_ref, k, x):
    nx, total = v_ref.shape[1], None
    for s, w in WEIGHTS.items():
        diff = None
        if x + s < nx:
            diff = v_ref[k, x + s]
        if x - s >= 0:
            diff = -v_ref[k, x - s] if diff is None else diff - v_ref[k, x - s]
        if diff is not None:
            diff = diff if w == 1.0 else w * diff
            total = diff if total is None else total + diff
    return total


def own_rate(scale, keep, x, v_ref, base, vel_ref, c_ref, sponge_ref, gy, gz):
    part = scale / 60.0
    c, held = c_ref[x] * part, keep - sponge_ref[x] * scale
    acc = [base[k] + held * v_ref[k, x] for k in range(5)]
    gx = [x_difference(v_ref, k, x) for k in range(5)]
    for d, g in enumerate((gx, gy, gz)):
        acc = couple(acc, vel_ref[d, x] * part, c, d, g)
    return acc


def add_x_blocks(scale, out_ref, vel_ref, c_ref, x_blocks):
    nx = out_ref.shape[1]
    for ref, (above, present) in zip(x_blocks, x_sides()):
        keep = jnp.where(present, jnp.where(above, scale / 60.0, -scale / 60.0), 0.0)
        for e in range(HALO):
            x = jnp.where(above, nx - 1 - e, e)
            grad = []
            for k in range(5):
                total = None
                for m in range(HALO - e):
                    w = WEIGHTS[m + 1 + e]
                    term = ref[k, jnp.where(above, m, HALO - 1 - m)]
                    term = term if w == 1.0 else w * term
                    total = term if total is None else total + term
                grad.append(total)
            acc = couple([out_ref[k, x] for k in range(5)], vel_ref[0, x] * keep, c_ref[x] * keep, 0, grad)
            for k in range(5):
                out_ref[k, x] = acc[k]


def own_planes(scale, keep, v_ref, base_of, vel_ref, c_ref, sponge_ref, table_ref, z_blocks, out_ref, dy, dz):
    nx, ny, nz = v_ref.shape[1:]
    bands = Bands(table_ref, v_ref.shape[1:])
    ay, bz = bands.along_y(), bands.along_z()
    for k in range(5):
        high, low = halves(v_ref[k].reshape(nx * ny, nz))
        dy[k] = (dot(ay, high) + dot(ay, low)).reshape(nx, ny, nz)
        along_z = dot(jnp.concatenate([high, low], axis=1), bz)
        for ref, side in zip(z_blocks, sides_of("tz")):
            along_z = along_z + dot(stacked(ref[k].reshape(nx * ny, nz), 1), bands.from_z(side))
        dz[k] = along_z.reshape(nx, ny, nz)
    for x in range(nx):
        gy, gz = [dy[k, x] for k in range(5)], [dz[k, x] for k in range(5)]
        base = [base_of(k, x) for k in range(5)]
        acc = own_rate(scale, keep, x, v_ref, base, vel_ref, c_ref, sponge_ref, gy, gz)
        for k in range(5):
            out_ref[k, x] = acc[k]


def first_kernel(adj, vel, c, sponge, source, table, _, *refs):
    n_z, refs = len(sides_of("tz")), refs[2:]
    z_blocks, (out_ref, base_ref, face_ref, bands_ref, dy, dz) = refs[:n_z], refs[n_z:]
    face_ref[...] = sponge[:FACE_PLANES]
    bands_ref[...] = table[table.shape[0] - bands_ref.shape[0] :]

    def base_of(k, x):
        base_ref[k, x] = 0.5 * adj[k, x] + (0.5 * TIME_STEP) * source[k, x]
        return TIME_STEP * source[k, x]

    own_planes(TIME_STEP, 1.0, adj, base_of, vel, c, sponge, table, z_blocks, out_ref, dy, dz)


def second_kernel(mid, base, vel, c, sponge, table, *refs):
    n_z = len(sides_of("tz"))
    z_blocks, (out_ref, dy, dz) = refs[:n_z], refs[n_z:]
    base_of = lambda k, x: base[k, x]
    own_planes(0.5 * TIME_STEP, 0.5, mid, base_of, vel, c, sponge, table, z_blocks, out_ref, dy, dz)


def add_y_blocks(scale, out_ref, vel_ref, c_ref, y_blocks, edge_ref):
    nx, ny, nz = out_ref.shape[1:]
    size = nx * EDGE
    part = scale / 60.0
    for ref, side in zip(y_blocks, sides_of("ty")):
        values = [stacked(ref[k].reshape(HALO * nx, nz), 0) for k in range(5)]
        grads = dot(edge_ref[pl.ds(pl.multiple_of(side * size, 16), size), : 2 * HALO * nx], jnp.concatenate(values, axis=1))
        at = pl.multiple_of(jnp.where(side == ABOVE, ny - EDGE, 0), EDGE)
        for x in range(nx):
            rows = pl.ds(at, EDGE)
            grad = [grads[x * EDGE : (x + 1) * EDGE, k * nz : (k + 1) * nz] for k in range(5)]
            acc = [out_ref[k, x, rows, :] for k in range(5)]
            acc = couple(acc, vel_ref[1, x, rows, :] * part, c_ref[x, rows, :] * part, 1, grad)
            for k in range(5):
                out_ref[k, x, rows, :] = acc[k]


def mid_kernel(part_ref, vel, c, edge, *refs):
    n_y = len(sides_of("ty"))
    n_z = len(sides_of("tz"))
    x_blocks, y_blocks, (out_ref, *msgs) = refs[:2], refs[2 : 2 + n_y], refs[2 + n_y + n_z :]
    add_y_blocks(TIME_STEP, out_ref, vel, c, y_blocks, edge)
    add_x_blocks(TIME_STEP, out_ref, vel, c, x_blocks)
    pack_second(out_ref, msgs[:2], msgs[2:])


def sums_kernel(mid, base, vel, c, sponge, table, owner_ref, *refs):
    n_y, n_z = len(sides_of("ty")), len(sides_of("tz"))
    x_blocks, y_blocks, auxes, sums_ref = refs[:2], refs[2 : 2 + n_y], refs[2 + n_y : 2 + n_y + n_z], refs[-1]
    nx, ny, nz = mid.shape[1:]
    rows = FACE_PLANES * ny
    bands = Bands(table, mid.shape[1:], tables(*mid.shape[1:])[2]["bz"])
    scale = 0.5 * TIME_STEP
    part = scale / 60.0
    flat = lambda v: v.reshape(rows, nz)
    split = [halves(flat(mid[k, :FACE_PLANES])) for k in range(5)]
    tall = jnp.concatenate([jnp.concatenate(pair, axis=0) for pair in split], axis=1)
    wide = jnp.concatenate([jnp.concatenate(pair, axis=1) for pair in split], axis=0)
    along_y = lambda i: [g for g in jnp.split(dot(bands.face_y(i), tall), 5, axis=1)]
    along_z = lambda m: [g for g in jnp.split(dot(wide, m), 5, axis=0)]
    groups, owners = [], []
    gy = [g.reshape(FACE_PLANES, ny, nz) for g in along_y(0)]
    gz = [g.reshape(FACE_PLANES, ny, nz) for g in along_z(bands.along_z())]
    planes = [
        own_rate(
            scale, 0.5, p, mid, [base[k, p] for k in range(5)], vel, c, sponge, [g[p] for g in gy], [g[p] for g in gz]
        )
        for p in range(FACE_PLANES)
    ]
    groups.append([jnp.concatenate([planes[p][k] for p in range(FACE_PLANES)], axis=0) for k in range(5)])
    eye = lax.broadcasted_iota(jnp.int32, (rows, rows), 0) == lax.broadcasted_iota(jnp.int32, (rows, rows), 1)
    owners.append(jnp.sum(jnp.where(eye, owner_ref[...].astype(F32), 0.0), axis=1, keepdims=True))

    def neighbour(ref, d, keep, grad):
        n = ref.shape[0]
        groups.append(couple(None, flat(ref[n - 2, :2]) * keep, flat(ref[n - 1, :2]) * keep, d, grad))
        owners.append(jnp.concatenate([ref[n - 2, 2], ref[n - 1, 2]], axis=0)[:, :1])

    grad = []
    for k in range(5):
        at_plane = []
        for p in range(FACE_PLANES):
            total = None
            for l in range(p, HALO):
                w = WEIGHTS[HALO + p - l]
                term = mid[k, nx - HALO + l]
                term = term if w == 1.0 else w * term
                total = term if total is None else total + term
            at_plane.append(total)
        grad.append(jnp.concatenate(at_plane, axis=0))
    for ref, (above, present) in zip(x_blocks, x_sides()):
        neighbour(ref, 0, jnp.where(jnp.logical_and(above, present), -part, 0.0), grad)
    for ref, side in zip(y_blocks, sides_of("ty")):
        neighbour(ref, 1, part, along_y(1 + turned(side)))
    for ref, side in zip(auxes, sides_of("tz")):
        neighbour(ref, 2, part, along_z(bands.from_z(turned(side))))

    devices = sums_ref.shape[0]
    each = devices // lax.axis_size("ax")
    total = rows * len(groups)
    place = (lax.broadcasted_iota(jnp.int32, (total, devices), 1) // each).astype(F32)
    choose = (jnp.concatenate(owners, axis=0) == place).astype(F32).astype(BF16)
    choose = jnp.concatenate([choose, choose], axis=0)
    values = [stacked(jnp.concatenate([g[k] for g in groups], axis=0), 0) for k in range(5)]
    sums = lax.dot_general(
        choose, jnp.concatenate(values, axis=1), (((0,), (0,)), ((), ())), preferred_element_type=F32
    )
    sums_ref[...] = sums.reshape(sums_ref.shape)


def final_kernel(part_ref, vel, c, edge, *refs):
    n_y = len(sides_of("ty"))
    x_blocks, y_blocks, (work, out_ref, token, sems) = refs[:2], refs[2 : 2 + n_y], refs[2 + n_y :]
    nx = part_ref.shape[1]
    token[...] = jnp.zeros(token.shape, F32)
    scale = 0.5 * TIME_STEP
    add_y_blocks(scale, work, vel, c, y_blocks, edge)
    inner = pltpu.make_async_copy(work.at[:, HALO : nx - HALO], out_ref.at[:, HALO : nx - HALO], sems.at[0])
    inner.start()
    add_x_blocks(scale, work, vel, c, x_blocks)
    low = pltpu.make_async_copy(work.at[:, :HALO], out_ref.at[:, :HALO], sems.at[1])
    high = pltpu.make_async_copy(work.at[:, nx - HALO :], out_ref.at[:, nx - HALO :], sems.at[2])
    low.start()
    high.start()
    inner.wait()
    low.wait()
    high.wait()


def modes_kernel(scale, sums_ref, basis_ref, _, out_ref):
    share = out_ref.shape[2]
    total = sums_ref[0]
    for i in range(1, sums_ref.shape[0]):
        total = total + sums_ref[i]
    modes = lax.dot_general(
        jnp.concatenate(jnp.split(total, 5, axis=1), axis=0), basis_ref[0], (((1,), (0,)), ((), ())), precision=lax.Precision.HIGHEST, preferred_element_type=F32
    )
    mine = lax.axis_index("ty") * lax.axis_size("tz") + lax.axis_index("tz")
    width = modes.shape[1]
    modes = pltpu.roll(modes * scale, lax.rem(width - mine * share, width), 1)
    for k in range(5):
        out_ref[k] = modes[k : k + 1, :share]


def swap_x(first, second):
    count, cores = lax.axis_size("ax"), lax.axis_size("tz")
    if not pairs_of(count):
        return [ring(first, "ax", 1), ring(second, "ax", -1)]
    near = lax.ppermute(first, "ax", [(i, i ^ 1) for i in range(count)])
    pairs = []
    for i in range(count):
        for u in range(cores):
            if i in (0, count - 1):
                pairs.append((i * cores + u, i * cores + (u + 1) % cores))
            else:
                j = i - 1 if i % 2 == 0 else i + 1
                pairs.append((i * cores + u, j * cores + u))
    return [near, lax.ppermute(second, ("ax", "tz"), pairs)]


def ring(v, axis, step):
    count = lax.axis_size(axis)
    return lax.ppermute(v, axis, [(i, (i + step) % count) for i in range(count)])


def from_sides(axis, to_above, to_below):
    if lax.axis_size(axis) == 2:
        return [ring(to_above, axis, 1)]
    return [ring(to_above, axis, 1), ring(to_below, axis, -1)]


def call(kernel, args, outs, scratch=(), away={}, out_away={}, flops=0, grant=12, hint=(20, 10), same={}):
    moved = sum(4 * math.prod(a.shape) for a in (*args, *outs))
    return pl.pallas_call(
        kernel,
        out_shape=list(outs),
        in_specs=[away.get(i, VMEM) for i in range(len(args))],
        out_specs=[out_away.get(i, VMEM) for i in range(len(outs))],
        scratch_shapes=list(scratch),
        input_output_aliases=same,
        cost_estimate=pl.CostEstimate(flops=int(flops * hint[0]), bytes_accessed=int(moved * hint[1]), transcendentals=0),
        compiler_params=pltpu.CompilerParams(vmem_limit_bytes=grant << 20),
    )(*args)


def on_device(adjoint, velocity, sound_speed, sponge, source, mode_basis, block_owner):
    nx, ny, nz = adjoint.shape[1:]
    n_ax, n_ty, n_tz = (lax.axis_size(a) for a in ("ax", "ty", "tz"))
    n_y = 1 if n_ty == 2 else 2
    table, edge, places = tables(nx, ny, nz)
    shape = lambda *s: jax.ShapeDtypeStruct(s, F32)
    brick = shape(5, nx, ny, nz)
    grads = [pltpu.VMEM((5, nx, ny, nz), F32)] * 2
    work = 5 * nx * ny * nz * 800
    owners = block_owner.reshape(1, FACE_PLANES * ny)
    devices = n_ax * n_ty * n_tz

    *msgs, aux, token = call(
        pack_first,
        [adjoint, velocity, sound_speed, owners],
        [shape(7, HALO, ny, nz)] * 2 + [shape(7, HALO, nx, nz)] * n_y + [shape(2, HALO, ny, nz), shape(8, nz)],
        [pltpu.VMEM((n_y, 5, nx, 8, nz), F32), pltpu.VMEM((4, FACE_PLANES, ny, nz), F32), pltpu.VMEM(owners.shape, jnp.int32), pltpu.SemaphoreType.DMA((8,))],
        away={i: HBM for i in range(4)},
        grant=60, flops=10**6,
    )
    whole, _ = lax.optimization_barrier((adjoint, token))
    z_blocks = from_sides("tz", whole, whole)
    auxes = from_sides("tz", aux, aux)
    y_first = from_sides("ty", msgs[2], msgs[-1])
    x_first = swap_x(msgs[0], msgs[1])
    fields = [velocity, sound_speed, sponge, source, table]
    part, base, face_sponge, face_table = call(
        first_kernel, [adjoint, *fields, token, owners, edge, *z_blocks], [brick, brick, shape(FACE_PLANES, ny, nz), jax.ShapeDtypeStruct((table.shape[0] - places["bz"], nz), BF16)], grads, away={6: ANY}, flops=work, grant=8
    )
    vel, c = velocity, sound_speed
    mid, *msgs = call(
        mid_kernel,
        [part, vel, c, edge, *x_first, *y_first, *auxes],
        [brick] + [shape(5, HALO, ny, nz)] * 2 + [shape(5, HALO, nx, nz)] * n_y,
        flops=work // 4,
        same={0: 0},
        grant=8,
    )
    z_blocks = from_sides("tz", mid, mid)
    y_blocks = from_sides("ty", msgs[2], msgs[-1])
    x_blocks = swap_x(msgs[0], msgs[1])
    (sums,) = call(
        sums_kernel,
        [mid, base, vel, c, face_sponge, face_table, owners, *x_first, *y_first, *auxes],
        [shape(devices, 1, 5 * nz)],
        flops=work // 4,
        grant=8,
    )
    sums = lax.all_to_all(sums, ("ax", "ty", "tz"), split_axis=0, concat_axis=0, tiled=True)
    (part,) = call(
        second_kernel, [mid, base, vel, c, sponge, table, *z_blocks], [brick], grads, flops=work, grant=8
    )
    _, adjoint_out, token = call(
        final_kernel,
        [part, vel, c, edge, *x_blocks, *y_blocks],
        [brick, brick, shape(8, nz)],
        [pltpu.SemaphoreType.DMA((3,))],
        out_away={1: HBM},
        same={0: 0},
        flops=work // 4,
        grant=6,
    )
    share = mode_basis.shape[2] // (n_ty * n_tz)
    scale = 1.0 / math.sqrt(FACE_PLANES * ny * n_ty * n_tz)
    (modes,) = call(functools.partial(modes_kernel, scale), [sums, mode_basis, token], [shape(5, 1, share)], grant=2)
    return (adjoint_out, jnp.transpose(modes, (1, 0, 2)))


def solution(mesh):
    return jax.shard_map(
        on_device,
        mesh=mesh,
        in_specs=(
            P(None, "ax", "ty", "tz"),
            P(None, "ax", "ty", "tz"),
            P("ax", "ty", "tz"),
            P("ax", "ty", "tz"),
            P(None, "ax", "ty", "tz"),
            P("ax", None, None),
            P("ax", "ty", "tz", None, None),
        ),
        out_specs=(P(None, "ax", "ty", "tz"), P("ax", None, ("ty", "tz"))),
        check_vma=False,
    )
```

```python
import functools
import math

import jax
import jax.numpy as jnp
import numpy as np
from jax import lax
from jax.experimental import pallas as pl
from jax.experimental.pallas import tpu as pltpu
from jax.sharding import PartitionSpec as P

FACE_PLANES = 2
TIME_STEP = 0.6
HALO = 3
EDGE = 8
WEIGHTS = {1: 45.0, 2: -9.0, 3: 1.0}
F32, BF16 = jnp.float32, jnp.bfloat16
VMEM = pl.BlockSpec(memory_space=pltpu.VMEM)
ANY = pl.BlockSpec(memory_space=pl.ANY)
HBM = pl.BlockSpec(memory_space=pltpu.HBM)
ABOVE, BELOW, NONE = 0, 1, 2


def weight_of(offset):
    size = np.abs(offset)
    table = np.zeros(offset.shape, np.float32)
    for s, w in WEIGHTS.items():
        table = np.where(size == s, np.sign(offset) * w, table)
    return table


def tables(nx, ny, nz):
    sides_y, sides_z = (2 if lax.axis_size(axis) == 2 else 3 for axis in ("ty", "tz"))
    y, z, layer, x = np.arange(ny), np.arange(nz), np.arange(HALO), np.eye(nx, dtype=np.float32)
    face = np.eye(FACE_PLANES, dtype=np.float32)
    band = weight_of(y[None, :] - y[:, None])
    along_z = weight_of(z[:, None] - z[None, :])

    def from_rows(places, rows):
        w = weight_of(places[None, :] - rows[:, None])
        return np.einsum("xp,yl->xylp", x, w).reshape(nx * EDGE, HALO * nx)

    y_halo = [from_rows(ny + layer, y[ny - EDGE :]), from_rows(layer - HALO, y[:EDGE])]
    y_halo = np.stack(y_halo + [np.zeros((nx * EDGE, HALO * nx))])
    y_face = np.stack(
        [np.kron(face, weight_of(y[None, :] + o - y[:, None])) for o in (ny, -ny)]
        + [np.zeros((FACE_PLANES * ny, FACE_PLANES * ny))]
    )
    z_halo = np.stack([weight_of(z[:, None] + o - z[None, :]) for o in (nz, -nz)] + [np.zeros((nz, nz))])
    twice = lambda m, axis: np.concatenate([m, m], axis=axis)
    columns = lambda m: np.pad(m, [(0, 0)] * (m.ndim - 1) + [(0, -m.shape[-1] % nz)])
    parts = dict(
        ay=np.concatenate(np.split(np.kron(x, band), nx * ny // nz, axis=1)),
        bz=twice(along_z, 0),
        wz=twice(z_halo[:sides_z], 1).reshape(-1, nz),
        fy=columns(np.concatenate([twice(np.kron(face, band), 1)[None], twice(y_face[:sides_y], 2)])).reshape(-1, nz),
    )
    places, at = {}, 0
    for name, m in parts.items():
        places[name], at = at, at + m.shape[0]
    edge = columns(twice(y_halo[:sides_y], 2)).reshape(-1, nz)
    return jnp.asarray(np.concatenate(list(parts.values())), BF16), jnp.asarray(edge, BF16), places


class Bands:
    def __init__(self, ref, shape, skipped=0):
        self.ref, self.skipped, (self.nx, self.ny, self.nz) = ref, skipped, shape
        self.places = tables(*shape)[2]

    def block(self, name, rows, i=0, width=None):
        at = self.places[name] - self.skipped
        start = at + i * rows if isinstance(i, int) else pl.multiple_of(at + i * rows, 16)
        return self.ref[pl.ds(start, rows), : self.nz if width is None else width]

    def along_y(self):
        rows = self.nx * self.ny
        return jnp.concatenate([self.block("ay", rows, i) for i in range(rows // self.nz)], axis=1)

    def along_z(self):
        return self.block("bz", 2 * self.nz)

    def from_z(self, side):
        return self.block("wz", 2 * self.nz, side)

    def face_y(self, i):
        return self.block("fy", FACE_PLANES * self.ny, i, 2 * FACE_PLANES * self.ny)


def halves(v):
    high = v.astype(BF16)
    return high, (v - high.astype(F32)).astype(BF16)


def stacked(v, axis):
    return jnp.concatenate(halves(v), axis=axis)


def dot(a, b):
    return jnp.dot(a, b, preferred_element_type=F32)


def couple(acc, u, c, d, grad):
    acc = [u * grad[k] if acc is None else acc[k] + u * grad[k] for k in range(5)]
    acc[1 + d] = acc[1 + d] + c * grad[4]
    acc[4] = acc[4] + c * grad[1 + d]
    return acc


def pairs_of(count):
    return count % 2 == 0


def x_sides():
    at, count = lax.axis_index("ax"), lax.axis_size("ax")
    has_lo, has_hi = at > 0, at < count - 1
    if not pairs_of(count):
        return [(False, has_lo), (True, has_hi)]
    even = lax.rem(at, 2) == 0
    return [(even, jnp.where(even, has_hi, has_lo)), (jnp.logical_not(even), jnp.where(even, has_lo, has_hi))]


def sides_of(axis):
    at, count = lax.axis_index(axis), lax.axis_size(axis)
    if count == 2:
        return [at]
    return [jnp.where(at > 0, BELOW, NONE), jnp.where(at < count - 1, ABOVE, NONE)]


def turned(side):
    if isinstance(side, int):
        return (BELOW, ABOVE, NONE)[side]
    return jnp.where(side == NONE, NONE, 1 - side)


def start_of(from_above_next, size):
    if isinstance(from_above_next, bool):
        return size - HALO if from_above_next else 0
    return jnp.where(from_above_next, size - HALO, 0)


def pack_first(adj, vel, c, owner_ref, *refs):
    n_y = len(sides_of("ty"))
    x_msgs, y_msgs, (aux, token, rows, speeds, names, sems) = refs[:2], refs[2 : 2 + n_y], refs[2 + n_y :]
    nx, ny, nz = adj.shape[1:]
    half = rows.shape[3]
    at = lax.axis_index("ty")
    copies = []

    def copy(src, dst):
        copies.append(pltpu.make_async_copy(src, dst, sems.at[len(copies)]))
        copies[-1].start()

    if n_y == 1:
        tops = [at == 0]
    else:
        tops = [True, False]
    for i, top in enumerate(tops):
        first = (ny - half if top else 0) if isinstance(top, bool) else pl.multiple_of(jnp.where(top, ny - half, 0), 8)
        copy(adj.at[:, :, pl.ds(first, half), :], rows.at[i])
    for ref, (above, _) in zip(x_msgs, x_sides()):
        up = above if pairs_of(lax.axis_size("ax")) else not above
        copy(adj.at[:, pl.ds(start_of(up, nx), HALO)], ref.at[:5])
    copy(vel.at[:, :FACE_PLANES], speeds.at[:3])
    copy(c.at[:FACE_PLANES], speeds.at[3])
    copy(owner_ref, names)
    for one in copies[-3:]:
        one.wait()
    token[...] = jnp.zeros(token.shape, F32)
    blocks = names.shape[1]
    eye = lax.broadcasted_iota(jnp.int32, (blocks, blocks), 0) == lax.broadcasted_iota(jnp.int32, (blocks, blocks), 1)
    column = jnp.sum(jnp.where(eye, names[...].astype(F32), 0.0), axis=1, keepdims=True)
    owners = jnp.broadcast_to(column, (blocks, nz)).reshape(FACE_PLANES, ny, nz)
    for d, msgs in enumerate((x_msgs, y_msgs, (aux,))):
        for ref in msgs:
            n = ref.shape[0]
            ref[n - 2, :2] = speeds[d]
            ref[n - 1, :2] = speeds[3]
            ref[n - 2, 2] = owners[0]
            ref[n - 1, 2] = owners[1]
    for one in copies[:-3]:
        one.wait()
    for i, (ref, top) in enumerate(zip(y_msgs, tops)):

        def put(r, ref=ref, i=i):
            for k in range(5):
                for l in range(HALO):
                    ref[k, l] = rows[i, k, :, r + l, :]

        if isinstance(top, bool):
            put(half - HALO if top else 0)
        else:
            pl.when(top)(functools.partial(put, half - HALO))
            pl.when(jnp.logical_not(top))(functools.partial(put, 0))


def pack_second(v_ref, x_msgs, y_msgs):
    nx, ny = v_ref.shape[1:3]
    for ref, (above, _) in zip(x_msgs, x_sides()):
        up = above if pairs_of(lax.axis_size("ax")) else not above
        ref[...] = v_ref[:, pl.ds(start_of(up, nx), HALO)]

    def put(ref, start):
        for k in range(5):
            for l in range(HALO):
                ref[k, l] = v_ref[k, :, start + l, :]

    if len(y_msgs) == 1:
        at = lax.axis_index("ty")
        pl.when(at == 0)(functools.partial(put, y_msgs[0], ny - HALO))
        pl.when(at != 0)(functools.partial(put, y_msgs[0], 0))
    else:
        put(y_msgs[0], ny - HALO)
        put(y_msgs[1], 0)


def x_difference(v_ref, k, x):
    nx, total = v_ref.shape[1], None
    for s, w in WEIGHTS.items():
        diff = None
        if x + s < nx:
            diff = v_ref[k, x + s]
        if x - s >= 0:
            diff = -v_ref[k, x - s] if diff is None else diff - v_ref[k, x - s]
        if diff is not None:
            diff = diff if w == 1.0 else w * diff
            total = diff if total is None else total + diff
    return total


def own_rate(scale, keep, x, v_ref, base, vel_ref, c_ref, sponge_ref, gy, gz):
    part = scale / 60.0
    c, held = c_ref[x] * part, keep - sponge_ref[x] * scale
    acc = [base[k] + held * v_ref[k, x] for k in range(5)]
    gx = [x_difference(v_ref, k, x) for k in range(5)]
    for d, g in enumerate((gx, gy, gz)):
        acc = couple(acc, vel_ref[d, x] * part, c, d, g)
    return acc


def add_x_blocks(scale, out_ref, vel_ref, c_ref, x_blocks):
    nx = out_ref.shape[1]
    for ref, (above, present) in zip(x_blocks, x_sides()):
        keep = jnp.where(present, jnp.where(above, scale / 60.0, -scale / 60.0), 0.0)
        for e in range(HALO):
            x = jnp.where(above, nx - 1 - e, e)
            grad = []
            for k in range(5):
                total = None
                for m in range(HALO - e):
                    w = WEIGHTS[m + 1 + e]
                    term = ref[k, jnp.where(above, m, HALO - 1 - m)]
                    term = term if w == 1.0 else w * term
                    total = term if total is None else total + term
                grad.append(total)
            acc = couple([out_ref[k, x] for k in range(5)], vel_ref[0, x] * keep, c_ref[x] * keep, 0, grad)
            for k in range(5):
                out_ref[k, x] = acc[k]


def own_planes(scale, keep, v_ref, base_of, vel_ref, c_ref, sponge_ref, table_ref, z_blocks, out_ref, dy, dz):
    nx, ny, nz = v_ref.shape[1:]
    bands = Bands(table_ref, v_ref.shape[1:])
    ay, bz = bands.along_y(), bands.along_z()
    for k in range(5):
        high, low = halves(v_ref[k].reshape(nx * ny, nz))
        dy[k] = (dot(ay, high) + dot(ay, low)).reshape(nx, ny, nz)
        along_z = dot(jnp.concatenate([high, low], axis=1), bz)
        for ref, side in zip(z_blocks, sides_of("tz")):
            along_z = along_z + dot(stacked(ref[k].reshape(nx * ny, nz), 1), bands.from_z(side))
        dz[k] = along_z.reshape(nx, ny, nz)
    for x in range(nx):
        gy, gz = [dy[k, x] for k in range(5)], [dz[k, x] for k in range(5)]
        base = [base_of(k, x) for k in range(5)]
        acc = own_rate(scale, keep, x, v_ref, base, vel_ref, c_ref, sponge_ref, gy, gz)
        for k in range(5):
            out_ref[k, x] = acc[k]


def first_kernel(adj, vel, c, sponge, source, table, _, *refs):
    n_z, refs = len(sides_of("tz")), refs[2:]
    z_blocks, (out_ref, base_ref, face_ref, bands_ref, dy, dz) = refs[:n_z], refs[n_z:]
    face_ref[...] = sponge[:FACE_PLANES]
    bands_ref[...] = table[table.shape[0] - bands_ref.shape[0] :]

    def base_of(k, x):
        base_ref[k, x] = 0.5 * adj[k, x] + (0.5 * TIME_STEP) * source[k, x]
        return TIME_STEP * source[k, x]

    own_planes(TIME_STEP, 1.0, adj, base_of, vel, c, sponge, table, z_blocks, out_ref, dy, dz)


def second_kernel(mid, base, vel, c, sponge, table, *refs):
    n_z = len(sides_of("tz"))
    z_blocks, (out_ref, dy, dz) = refs[:n_z], refs[n_z:]
    base_of = lambda k, x: base[k, x]
    own_planes(0.5 * TIME_STEP, 0.5, mid, base_of, vel, c, sponge, table, z_blocks, out_ref, dy, dz)


def add_y_blocks(scale, out_ref, vel_ref, c_ref, y_blocks, edge_ref):
    nx, ny, nz = out_ref.shape[1:]
    size = nx * EDGE
    part = scale / 60.0
    for ref, side in zip(y_blocks, sides_of("ty")):
        values = [stacked(ref[k].reshape(HALO * nx, nz), 0) for k in range(5)]
        grads = dot(edge_ref[pl.ds(pl.multiple_of(side * size, 16), size), : 2 * HALO * nx], jnp.concatenate(values, axis=1))
        at = pl.multiple_of(jnp.where(side == ABOVE, ny - EDGE, 0), EDGE)
        for x in range(nx):
            rows = pl.ds(at, EDGE)
            grad = [grads[x * EDGE : (x + 1) * EDGE, k * nz : (k + 1) * nz] for k in range(5)]
            acc = [out_ref[k, x, rows, :] for k in range(5)]
            acc = couple(acc, vel_ref[1, x, rows, :] * part, c_ref[x, rows, :] * part, 1, grad)
            for k in range(5):
                out_ref[k, x, rows, :] = acc[k]


def mid_kernel(part_ref, vel, c, edge, *refs):
    n_y = len(sides_of("ty"))
    n_z = len(sides_of("tz"))
    x_blocks, y_blocks, (out_ref, *msgs) = refs[:2], refs[2 : 2 + n_y], refs[2 + n_y + n_z :]
    out_ref[...] = part_ref[...]
    add_y_blocks(TIME_STEP, out_ref, vel, c, y_blocks, edge)
    add_x_blocks(TIME_STEP, out_ref, vel, c, x_blocks)
    pack_second(out_ref, msgs[:2], msgs[2:])


def sums_kernel(mid, base, vel, c, sponge, table, owner_ref, *refs):
    n_y, n_z = len(sides_of("ty")), len(sides_of("tz"))
    x_blocks, y_blocks, auxes, sums_ref = refs[:2], refs[2 : 2 + n_y], refs[2 + n_y : 2 + n_y + n_z], refs[-1]
    nx, ny, nz = mid.shape[1:]
    rows = FACE_PLANES * ny
    bands = Bands(table, mid.shape[1:], tables(*mid.shape[1:])[2]["bz"])
    scale = 0.5 * TIME_STEP
    part = scale / 60.0
    flat = lambda v: v.reshape(rows, nz)
    split = [halves(flat(mid[k, :FACE_PLANES])) for k in range(5)]
    tall = jnp.concatenate([jnp.concatenate(pair, axis=0) for pair in split], axis=1)
    wide = jnp.concatenate([jnp.concatenate(pair, axis=1) for pair in split], axis=0)
    along_y = lambda i: [g for g in jnp.split(dot(bands.face_y(i), tall), 5, axis=1)]
    along_z = lambda m: [g for g in jnp.split(dot(wide, m), 5, axis=0)]
    groups, owners = [], []
    gy = [g.reshape(FACE_PLANES, ny, nz) for g in along_y(0)]
    gz = [g.reshape(FACE_PLANES, ny, nz) for g in along_z(bands.along_z())]
    planes = [
        own_rate(
            scale, 0.5, p, mid, [base[k, p] for k in range(5)], vel, c, sponge, [g[p] for g in gy], [g[p] for g in gz]
        )
        for p in range(FACE_PLANES)
    ]
    groups.append([jnp.concatenate([planes[p][k] for p in range(FACE_PLANES)], axis=0) for k in range(5)])
    eye = lax.broadcasted_iota(jnp.int32, (rows, rows), 0) == lax.broadcasted_iota(jnp.int32, (rows, rows), 1)
    owners.append(jnp.sum(jnp.where(eye, owner_ref[...].astype(F32), 0.0), axis=1, keepdims=True))

    def neighbour(ref, d, keep, grad):
        n = ref.shape[0]
        groups.append(couple(None, flat(ref[n - 2, :2]) * keep, flat(ref[n - 1, :2]) * keep, d, grad))
        owners.append(jnp.concatenate([ref[n - 2, 2], ref[n - 1, 2]], axis=0)[:, :1])

    grad = []
    for k in range(5):
        at_plane = []
        for p in range(FACE_PLANES):
            total = None
            for l in range(p, HALO):
                w = WEIGHTS[HALO + p - l]
                term = mid[k, nx - HALO + l]
                term = term if w == 1.0 else w * term
                total = term if total is None else total + term
            at_plane.append(total)
        grad.append(jnp.concatenate(at_plane, axis=0))
    for ref, (above, present) in zip(x_blocks, x_sides()):
        neighbour(ref, 0, jnp.where(jnp.logical_and(above, present), -part, 0.0), grad)
    for ref, side in zip(y_blocks, sides_of("ty")):
        neighbour(ref, 1, part, along_y(1 + turned(side)))
    for ref, side in zip(auxes, sides_of("tz")):
        neighbour(ref, 2, part, along_z(bands.from_z(turned(side))))

    devices = sums_ref.shape[0]
    each = devices // lax.axis_size("ax")
    total = rows * len(groups)
    place = (lax.broadcasted_iota(jnp.int32, (total, devices), 1) // each).astype(F32)
    choose = (jnp.concatenate(owners, axis=0) == place).astype(F32).astype(BF16)
    choose = jnp.concatenate([choose, choose], axis=0)
    values = [stacked(jnp.concatenate([g[k] for g in groups], axis=0), 0) for k in range(5)]
    sums = lax.dot_general(
        choose, jnp.concatenate(values, axis=1), (((0,), (0,)), ((), ())), preferred_element_type=F32
    )
    sums_ref[...] = sums.reshape(sums_ref.shape)


def final_kernel(part_ref, vel, c, edge, *refs):
    n_y = len(sides_of("ty"))
    x_blocks, y_blocks, (out_ref, token, work, sems) = refs[:2], refs[2 : 2 + n_y], refs[2 + n_y :]
    nx = part_ref.shape[1]
    token[...] = jnp.zeros(token.shape, F32)
    scale = 0.5 * TIME_STEP
    work[...] = part_ref[...]
    add_y_blocks(scale, work, vel, c, y_blocks, edge)
    inner = pltpu.make_async_copy(work.at[:, HALO : nx - HALO], out_ref.at[:, HALO : nx - HALO], sems.at[0])
    inner.start()
    add_x_blocks(scale, work, vel, c, x_blocks)
    low = pltpu.make_async_copy(work.at[:, :HALO], out_ref.at[:, :HALO], sems.at[1])
    high = pltpu.make_async_copy(work.at[:, nx - HALO :], out_ref.at[:, nx - HALO :], sems.at[2])
    low.start()
    high.start()
    inner.wait()
    low.wait()
    high.wait()


def modes_kernel(scale, sums_ref, basis_ref, _, out_ref):
    share = out_ref.shape[2]
    total = sums_ref[0]
    for i in range(1, sums_ref.shape[0]):
        total = total + sums_ref[i]
    parts = halves(jnp.concatenate(jnp.split(total, 5, axis=1), axis=0))
    basis_high, basis_low = halves(basis_ref[0])
    modes = dot(
        jnp.concatenate([*parts, *parts], axis=1),
        jnp.concatenate([basis_high, basis_high, basis_low, basis_low], axis=0),
    )
    mine = lax.axis_index("ty") * lax.axis_size("tz") + lax.axis_index("tz")
    width = modes.shape[1]
    modes = pltpu.roll(modes * scale, lax.rem(width - mine * share, width), 1)
    for k in range(5):
        out_ref[k] = modes[k : k + 1, :share]


def swap_x(first, second):
    count, cores = lax.axis_size("ax"), lax.axis_size("tz")
    if not pairs_of(count):
        return [ring(first, "ax", 1), ring(second, "ax", -1)]
    near = lax.ppermute(first, "ax", [(i, i ^ 1) for i in range(count)])
    pairs = []
    for i in range(count):
        for u in range(cores):
            if i in (0, count - 1):
                pairs.append((i * cores + u, i * cores + (u + 1) % cores))
            else:
                j = i - 1 if i % 2 == 0 else i + 1
                pairs.append((i * cores + u, j * cores + u))
    return [near, lax.ppermute(second, ("ax", "tz"), pairs)]


def ring(v, axis, step):
    count = lax.axis_size(axis)
    return lax.ppermute(v, axis, [(i, (i + step) % count) for i in range(count)])


def from_sides(axis, to_above, to_below):
    if lax.axis_size(axis) == 2:
        return [ring(to_above, axis, 1)]
    return [ring(to_above, axis, 1), ring(to_below, axis, -1)]


def call(kernel, args, outs, scratch=(), away={}, out_away={}, flops=0, grant=12, hint=(20, 10)):
    moved = sum(4 * math.prod(a.shape) for a in (*args, *outs))
    return pl.pallas_call(
        kernel,
        out_shape=list(outs),
        in_specs=[away.get(i, VMEM) for i in range(len(args))],
        out_specs=[out_away.get(i, VMEM) for i in range(len(outs))],
        scratch_shapes=list(scratch),
        cost_estimate=pl.CostEstimate(flops=int(flops * hint[0]), bytes_accessed=int(moved * hint[1]), transcendentals=0),
        compiler_params=pltpu.CompilerParams(vmem_limit_bytes=grant << 20),
    )(*args)


def on_device(adjoint, velocity, sound_speed, sponge, source, mode_basis, block_owner):
    nx, ny, nz = adjoint.shape[1:]
    n_ax, n_ty, n_tz = (lax.axis_size(a) for a in ("ax", "ty", "tz"))
    n_y = 1 if n_ty == 2 else 2
    table, edge, places = tables(nx, ny, nz)
    shape = lambda *s: jax.ShapeDtypeStruct(s, F32)
    brick = shape(5, nx, ny, nz)
    grads = [pltpu.VMEM((5, nx, ny, nz), F32)] * 2
    work = 5 * nx * ny * nz * 800
    owners = block_owner.reshape(1, FACE_PLANES * ny)
    devices = n_ax * n_ty * n_tz

    *msgs, aux, token = call(
        pack_first,
        [adjoint, velocity, sound_speed, owners],
        [shape(7, HALO, ny, nz)] * 2 + [shape(7, HALO, nx, nz)] * n_y + [shape(2, HALO, ny, nz), shape(8, nz)],
        [pltpu.VMEM((n_y, 5, nx, 8, nz), F32), pltpu.VMEM((4, FACE_PLANES, ny, nz), F32), pltpu.VMEM(owners.shape, jnp.int32), pltpu.SemaphoreType.DMA((8,))],
        away={i: HBM for i in range(4)},
        grant=60, flops=10**6,
    )
    z_blocks = from_sides("tz", adjoint, adjoint)
    auxes = from_sides("tz", aux, aux)
    y_first = from_sides("ty", msgs[2], msgs[-1])
    x_first = swap_x(msgs[0], msgs[1])
    fields = [velocity, sound_speed, sponge, source, table]
    part, base, face_sponge, face_table = call(
        first_kernel, [adjoint, *fields, token, owners, edge, *z_blocks], [brick, brick, shape(FACE_PLANES, ny, nz), jax.ShapeDtypeStruct((table.shape[0] - places["bz"], nz), BF16)], grads, away={6: ANY}, flops=work, grant=8
    )
    vel, c = velocity, sound_speed
    mid, *msgs = call(
        mid_kernel,
        [part, vel, c, edge, *x_first, *y_first, *auxes],
        [brick] + [shape(5, HALO, ny, nz)] * 2 + [shape(5, HALO, nx, nz)] * n_y,
        flops=work // 4,
        grant=8,
    )
    z_blocks = from_sides("tz", mid, mid)
    y_blocks = from_sides("ty", msgs[2], msgs[-1])
    x_blocks = swap_x(msgs[0], msgs[1])
    (sums,) = call(
        sums_kernel,
        [mid, base, vel, c, face_sponge, face_table, owners, *x_first, *y_first, *auxes],
        [shape(devices, 1, 5 * nz)],
        flops=work // 4,
        grant=8,
    )
    sums = lax.all_to_all(sums, ("ax", "ty", "tz"), split_axis=0, concat_axis=0, tiled=True)
    (part,) = call(
        second_kernel, [mid, base, vel, c, sponge, table, *z_blocks], [brick], grads, flops=work, grant=8
    )
    adjoint_out, token = call(
        final_kernel,
        [part, vel, c, edge, *x_blocks, *y_blocks],
        [brick, shape(8, nz)],
        [pltpu.VMEM((5, nx, ny, nz), F32), pltpu.SemaphoreType.DMA((3,))],
        out_away={0: HBM},
        flops=work // 4,
        grant=6,
    )
    share = mode_basis.shape[2] // (n_ty * n_tz)
    scale = 1.0 / math.sqrt(FACE_PLANES * ny * n_ty * n_tz)
    (modes,) = call(functools.partial(modes_kernel, scale), [sums, mode_basis, token], [shape(5, 1, share)], grant=2)
    return (adjoint_out, jnp.transpose(modes, (1, 0, 2)))


def solution(mesh):
    return jax.shard_map(
        on_device,
        mesh=mesh,
        in_specs=(
            P(None, "ax", "ty", "tz"),
            P(None, "ax", "ty", "tz"),
            P("ax", "ty", "tz"),
            P("ax", "ty", "tz"),
            P(None, "ax", "ty", "tz"),
            P("ax", None, None),
            P("ax", "ty", "tz", None, None),
        ),
        out_specs=(P(None, "ax", "ty", "tz"), P("ax", None, ("ty", "tz"))),
        check_vma=False,
    )
```
